512 devices in a mesh: seq: 64 (over y, z), tp: 8 (over x, core).
Axes of the slice: x: 4, y: 8, z: 8, core: 2. Of those that a mesh axis runs over, the one named last changes fastest.
Arguments:
- queries: bfloat16 [16384, 4096], P('seq', 'tp'), may hold values from -6 to 6
- keys: bfloat16 [16384, 4096], P('seq', 'tp'), may hold values from -6 to 6
- values: bfloat16 [16384, 4096], P('seq', 'tp'), may hold values from -6 to 6
- out_cotangent: bfloat16 [16384, 2048], P('seq', 'tp'), may hold values from -16 to 16
- proj_weight: bfloat16 [4096, 2048], P('tp', 'seq'), may hold values from -0.125 to 0.125
Outputs:
- grad_queries: bfloat16 [16384, 4096], P('seq', 'tp')
- grad_keys: bfloat16 [16384, 4096], P('seq', 'tp')
- grad_values: bfloat16 [16384, 4096], P('seq', 'tp')
- grad_proj: float32 [4096, 2048], P('tp', 'seq')
The draws below stay inside these ranges and needn't reach their ends.
All inputs are finite; a program needn't handle non-finite values.
Results may differ from the reference program's by a relative error of at most 0.0058.
Values may be sent and summed in bfloat16 or wider, within the bound.
No kernel may reach another device: no remote copies, remote signals or barrier semaphores. Data moves between devices by JAX's collectives and lax.ppermute only.
A program may use at most 128 MiB of HBM per device.

```python
import jax
import jax.numpy as jnp
from jax import lax

H = 32
DH = 128
COLS = 2048
TOK_DEV = 256
TOKENS = 16384
HD = 4096
N_SEQ = 64


def raised(result, rng, source, target, parts, factor):
    def block_of(position):
        return (jnp.arange(result.shape[position]) // (result.shape[position] // parts)).reshape((-1,) + (1,) * (result.ndim - 1 - position))

    near = jax.random.permutation(rng, parts)[block_of(target)]
    other_side = (block_of(target) + parts // 2) % parts
    return jnp.where((block_of(source) == near) | (block_of(source) == other_side), factor * result, result)


def block_scale(key, extent, pieces, low, top_value):
    def one(dim, parts):
        steps = jax.random.uniform(jax.random.fold_in(jax.random.fold_in(key, 6), dim), (parts,), jnp.float32, low / len(pieces), top_value / len(pieces))
        return jnp.repeat(jnp.exp(steps), extent[dim] // parts).reshape((-1,) + (1,) * (len(extent) - dim - 1))

    factor_of = one(*pieces[0])
    for cut in pieces[1:]:
        factor_of = factor_of * one(*cut)
    return factor_of


def normal_values(stream_key, dims, width, bound, shards=(), dtype=jnp.bfloat16):
    array = width * jax.random.normal(stream_key, dims, jnp.float32)
    if shards:
        array = array * block_scale(stream_key, dims, shards, -0.22, 0.18)
    return jnp.clip(array, -bound, bound).astype(dtype)


def heavy_noise(stream_key, dims, width, limit, split, heavy, kind=jnp.bfloat16):
    entries = width * jax.random.normal(stream_key, dims, jnp.float32)
    if split:
        entries = entries * block_scale(stream_key, dims, split, -0.22, 0.18)
    return jnp.clip(raised(entries, jax.random.fold_in(stream_key, 3), *heavy), -limit, limit).astype(kind)


def setup_inputs(seed: int = 0) -> dict:
    seeds = jax.random.split(jax.random.key(seed), 6)
    return {
        "queries": normal_values(seeds[0], (TOKENS, HD), 1.0, 6.0, ((0, 64), (1, 8))),
        "keys": normal_values(seeds[1], (TOKENS, HD), 1.0, 6.0, ((0, 64), (1, 8))),
        "values": normal_values(seeds[2], (TOKENS, HD), 1.0, 6.0, ((0, 64), (1, 8))),
        "out_cotangent": heavy_noise(seeds[3], (TOKENS, COLS), 1.0, 16.0, ((0, 64), (1, 8)), (0, 1, 64, 4.0)),
        "proj_weight": normal_values(seeds[4], (HD, COLS), COLS ** -0.5, 0.125, ((0, 8), (1, 64))),
    }


def reference(queries, keys, values, out_cotangent, proj_weight):
    blocks = N_SEQ
    scale = 1.0 / jnp.sqrt(jnp.float32(DH * TOKENS))
    q_blk = queries.reshape(blocks, TOK_DEV, H, DH)
    k_blk = keys.reshape(blocks, TOK_DEV, H, DH)
    v_blk = values.reshape(blocks, TOK_DEV, H, DH)
    grad_out = jnp.dot(out_cotangent, proj_weight.T, preferred_element_type=jnp.float32).astype(jnp.bfloat16)
    g_blk = grad_out.reshape(blocks, TOK_DEV, H, DH)
    kv_state = jnp.einsum('bthd,bthe->bhde', k_blk.astype(jnp.float32), v_blk.astype(jnp.float32))
    qg_state = jnp.einsum('bthd,bthe->bhde', q_blk.astype(jnp.float32), g_blk.astype(jnp.float32))
    zeros = jnp.zeros((1, H, DH, DH), jnp.float32)
    prior = jnp.concatenate([zeros, jnp.cumsum(kv_state, axis=0)[:-1]], axis=0).astype(jnp.bfloat16)
    rev = jnp.cumsum(qg_state[::-1], axis=0)[::-1]
    later = jnp.concatenate([rev[1:], zeros], axis=0).astype(jnp.bfloat16)
    rows = jnp.arange(TOK_DEV)
    causal = rows[:, None] >= rows[None, :]

    def one_block(items):
        q, k, v, g, pr, la = items
        qf = q.astype(jnp.float32)
        kf = k.astype(jnp.float32)
        vf = v.astype(jnp.float32)
        gf = g.astype(jnp.float32)
        prf = pr.astype(jnp.float32)
        laf = la.astype(jnp.float32)
        attn = jnp.where(causal[None], jnp.einsum('thd,shd->hts', qf, kf), 0.0).astype(jnp.bfloat16).astype(jnp.float32)
        back = jnp.where(causal[None], jnp.einsum('thd,shd->hts', gf, vf), 0.0).astype(jnp.bfloat16).astype(jnp.float32)
        out = scale * (jnp.einsum('hts,she->the', attn, vf) + jnp.einsum('thd,hde->the', qf, prf))
        dq = scale * (jnp.einsum('hts,shd->thd', back, kf) + jnp.einsum('the,hde->thd', gf, prf))
        dk = scale * (jnp.einsum('hts,thd->shd', back, qf) + jnp.einsum('she,hde->shd', vf, laf))
        dv = scale * (jnp.einsum('hts,the->she', attn, gf) + jnp.einsum('shd,hde->she', kf, laf))
        return (out.astype(jnp.bfloat16), dq.astype(jnp.bfloat16), dk.astype(jnp.bfloat16), dv.astype(jnp.bfloat16))
    out, dq, dk, dv = lax.map(one_block, (q_blk, k_blk, v_blk, g_blk, prior, later))
    attn_out = out.reshape(TOKENS, HD)
    grad_proj = jnp.dot(attn_out.T, out_cotangent, preferred_element_type=jnp.float32) / jnp.sqrt(jnp.float32(TOKENS))
    return (dq.reshape(TOKENS, HD), dk.reshape(TOKENS, HD), dv.reshape(TOKENS, HD), grad_proj)
```

```python
import jax
import jax.numpy as jnp
from jax import lax
from jax.experimental import pallas as pl
from jax.experimental.pallas import tpu as pltpu
from jax.sharding import Mesh, PartitionSpec as P

DH = 128
SEQ = ("y", "z")
BF16 = jnp.bfloat16
F32 = jnp.float32


def gather_by_exchange(part, axis):
    count = lax.axis_size(axis)
    copies = jnp.broadcast_to(part[None], (count,) + part.shape)
    return lax.all_to_all(copies, axis, 0, 0, tiled=True)


def running_kernel(reverse, parts_ref, sums_ref):
    count = parts_ref.shape[0]
    total = jnp.zeros(parts_ref.shape[1:], F32)
    for step in range(count):
        at = count - 1 - step if reverse else step
        sums_ref[at] = total.astype(sums_ref.dtype)
        total = total + parts_ref[at].astype(F32)


def entering(state, reverse):
    count = lax.axis_size(SEQ)
    heads, rows, cols = state.shape
    pieces = state.astype(BF16).reshape(count, heads * rows // count, cols)
    mine = lax.all_to_all(pieces, SEQ, 0, 0, tiled=True)
    sums = pl.pallas_call(
        lambda i, o: running_kernel(reverse, i, o),
        out_shape=jax.ShapeDtypeStruct(mine.shape, BF16),
    )(mine)
    back = lax.all_to_all(sums, SEQ, 0, 0, tiled=True)
    return back.reshape(heads, rows, cols)


def dot(spec, a, b):
    return jnp.einsum(spec, a, b, preferred_element_type=F32)


def per_device(queries, keys, values, out_cotangent, proj_weight):
    tok = queries.shape[0]
    heads = queries.shape[1] // DH
    seq_count = lax.axis_size(SEQ)
    scale = 1.0 / jnp.sqrt(F32(DH * tok * seq_count))
    q_heads = queries.reshape(tok, heads, DH)
    k_heads = keys.reshape(tok, heads, DH)
    v_heads = values.reshape(tok, heads, DH)
    weight_z = gather_by_exchange(proj_weight.T, "z")
    weight_t = lax.all_gather(weight_z, "y", axis=0, tiled=True)
    kv_state = dot("thd,the->hde", k_heads, v_heads)
    prior = entering(kv_state, False)
    full_cot = gather_by_exchange(out_cotangent, "tp")
    count_tp, _, cols = full_cot.shape
    weight_t = weight_t.reshape(count_tp, cols, heads * DH)
    grad_out = dot("ptc,pcd->td", full_cot, weight_t).astype(BF16)
    g_heads = grad_out.reshape(tok, heads, DH)
    qg_state = dot("thd,the->hde", q_heads, g_heads)
    later = entering(qg_state, True)
    rows = jnp.arange(tok)
    causal = (rows[:, None] >= rows[None, :])[None]
    attn = jnp.where(causal, dot("thd,shd->hts", q_heads, k_heads), 0.0).astype(BF16)
    back = jnp.where(causal, dot("thd,shd->hts", g_heads, v_heads), 0.0).astype(BF16)
    attn_out = scale * (dot("hts,she->the", attn, v_heads) + dot("thd,hde->the", q_heads, prior))
    grad_q = scale * (dot("hts,shd->thd", back, k_heads) + dot("the,hde->thd", g_heads, prior))
    grad_k = scale * (dot("hts,thd->shd", back, q_heads) + dot("she,hde->shd", v_heads, later))
    grad_v = scale * (dot("hts,the->she", attn, g_heads) + dot("shd,hde->she", k_heads, later))
    width = heads * DH
    out_flat = attn_out.astype(BF16).reshape(tok, width)
    proj_term = dot("ptc,td->pcd", full_cot, out_flat).astype(BF16)
    proj_parts = lax.all_to_all(
        proj_term.reshape(seq_count, -1, width), SEQ, 0, 0, tiled=True
    )
    proj_sum = jnp.sum(proj_parts.astype(F32), axis=0)
    grad_proj = (proj_sum / jnp.sqrt(F32(tok * seq_count))).T
    return (
        grad_q.astype(BF16).reshape(tok, width),
        grad_k.astype(BF16).reshape(tok, width),
        grad_v.astype(BF16).reshape(tok, width),
        grad_proj,
    )


def solution(mesh):
    seq, tp = mesh.devices.shape
    inner = 8
    grid = Mesh(mesh.devices.reshape(seq // inner, inner, tp), ("y", "z", "tp"))
    tokens, weight = P(SEQ, "tp"), P("tp", SEQ)
    return jax.shard_map(
        per_device,
        mesh=grid,
        in_specs=(tokens, tokens, tokens, tokens, weight),
        out_specs=(tokens, tokens, tokens, weight),
        check_vma=False,
    )
```

```python
import functools

import jax
import jax.numpy as jnp
from jax import lax
from jax.experimental import pallas as pl
from jax.experimental.pallas import tpu as pltpu
from jax.sharding import Mesh, PartitionSpec as P

DH = 128
SEQ = ("y", "z")
BF16 = jnp.bfloat16
F32 = jnp.float32
VMEM_BYTES = 48 * 1024 * 1024


def mm(a, b, ca, cb):
    return lax.dot_general(a, b, (((ca,), (cb,)), ((), ())), preferred_element_type=F32)


def head(h):
    return slice(h * DH, (h + 1) * DH)


def local_call(kernel, out_shape, flops, moved, **kwargs):
    return pl.pallas_call(
        kernel,
        out_shape=out_shape,
        cost_estimate=pl.CostEstimate(flops=flops, transcendentals=0, bytes_accessed=moved),
        compiler_params=pltpu.CompilerParams(vmem_limit_bytes=VMEM_BYTES),
        **kwargs,
    )


def causal(tok):
    rows = lax.broadcasted_iota(jnp.int32, (tok, tok), 0)
    cols = lax.broadcasted_iota(jnp.int32, (tok, tok), 1)
    return rows >= cols


def exchange(x, axis):
    return lax.all_to_all(x, axis, 0, 0, tiled=True)


def first_kernel(k_ref, v_ref, w_ref, out_ref):
    peers, rows, width = out_ref.shape
    own = w_ref.shape[0]
    share = rows - own
    for h in range(width // DH):
        kv = mm(k_ref[:, head(h)], v_ref[:, head(h)], 0, 0).astype(BF16)
        for p in range(peers):
            out_ref[p, own:, head(h)] = kv[p * share : (p + 1) * share]
    for p in range(peers):
        out_ref[p, :own, :] = w_ref[...]


def split_kernel(got_ref, weight_ref, part_ref, total_ref):
    peers, rows, width = got_ref.shape
    own = weight_ref.shape[0] // peers
    running = jnp.zeros((rows - own, width), F32)
    for p in range(peers):
        weight_ref[p * own : (p + 1) * own, :] = got_ref[p, :own, :]
        part_ref[p] = running
        running = running + got_ref[p, own:, :].astype(F32)
    for p in range(total_ref.shape[0]):
        total_ref[p] = running


def back_scan_kernel(got_ref, part_ref, total_ref):
    peers, rows, width = got_ref.shape
    running = jnp.zeros((rows, width), F32)
    for p in reversed(range(peers)):
        part_ref[p] = running
        running = running + got_ref[p].astype(F32)
    for p in range(total_ref.shape[0]):
        total_ref[p] = running


def join_kernel(reverse, place_ref, totals_ref, part_ref, out_ref):
    place = place_ref[0]
    base = jnp.zeros(totals_ref.shape[1:], F32)
    for other in range(totals_ref.shape[0]):
        counts = place < other if reverse else place > other
        base = base + jnp.where(counts, totals_ref[other], 0.0)
    for p in range(part_ref.shape[0]):
        out_ref[p] = (base + part_ref[p]).astype(out_ref.dtype)


def attn_kernel(q_ref, k_ref, v_ref, attn_ref, inner_ref):
    mask = causal(q_ref.shape[0])
    for h in range(q_ref.shape[1] // DH):
        scores = mm(q_ref[:, head(h)], k_ref[:, head(h)], 1, 1)
        attn = jnp.where(mask, scores, 0.0).astype(BF16)
        attn_ref[h] = attn
        inner_ref[:, head(h)] = mm(attn, v_ref[:, head(h)], 1, 0)


def proj_kernel(scale, q_ref, prior_ref, inner_ref, cot_ref, out_ref, attn_out_ref):
    @pl.when(pl.program_id(0) == 0)
    def _():
        for h in range(q_ref.shape[1] // DH):
            far = mm(q_ref[:, head(h)], prior_ref[:, head(h)], 1, 0)
            attn_out_ref[:, head(h)] = (scale * (inner_ref[:, head(h)] + far)).astype(BF16)

    out_ref[...] = mm(cot_ref[0], attn_out_ref[...], 0, 0)


def grad_out_kernel(cot_ref, w_ref, q_ref, g_ref, qg_ref, acc_ref):
    step = pl.program_id(0)
    term = mm(cot_ref[0], w_ref[...], 1, 0)

    @pl.when(step == 0)
    def _():
        acc_ref[...] = term

    @pl.when(step > 0)
    def _():
        acc_ref[...] += term

    @pl.when(step == pl.num_programs(0) - 1)
    def _():
        g = acc_ref[...].astype(BF16)
        g_ref[...] = g
        for h in range(g.shape[1] // DH):
            qg_ref[:, head(h)] = mm(q_ref[:, head(h)], g[:, head(h)], 0, 0).astype(BF16)


def inner_grads_kernel(scale, q_ref, k_ref, v_ref, g_ref, attn_ref, prior_ref, dq_ref, dk_ref, dv_ref):
    mask = causal(q_ref.shape[0])
    for h in range(q_ref.shape[1] // DH):
        g = g_ref[:, head(h)]
        back = jnp.where(mask, mm(g, v_ref[:, head(h)], 1, 1), 0.0).astype(BF16)
        near = mm(back, k_ref[:, head(h)], 1, 0)
        far = mm(g, prior_ref[:, head(h)], 1, 1)
        dq_ref[:, head(h)] = (scale * (near + far)).astype(BF16)
        dk_ref[:, head(h)] = mm(back, q_ref[:, head(h)], 0, 0)
        dv_ref[:, head(h)] = mm(attn_ref[h], g, 0, 0)


def outer_grads_kernel(scale, k_ref, v_ref, later_ref, near_k_ref, near_v_ref, dk_ref, dv_ref):
    for h in range(k_ref.shape[1] // DH):
        later = later_ref[:, head(h)]
        far_k = mm(v_ref[:, head(h)], later, 1, 1)
        dk_ref[:, head(h)] = (scale * (near_k_ref[:, head(h)] + far_k)).astype(BF16)
        far_v = mm(k_ref[:, head(h)], later, 1, 0)
        dv_ref[:, head(h)] = (scale * (near_v_ref[:, head(h)] + far_v)).astype(BF16)


def shape(dims, dtype):
    return jax.ShapeDtypeStruct(dims, dtype)


def join(place, totals, part, reverse):
    return local_call(
        functools.partial(join_kernel, reverse),
        shape(part.shape, BF16),
        0,
        3 * part.size * 4,
        in_specs=[
            pl.BlockSpec(memory_space=pltpu.SMEM),
            pl.BlockSpec(memory_space=pltpu.VMEM),
            pl.BlockSpec(memory_space=pltpu.VMEM),
        ],
    )(place, totals, part)


def per_device(queries, keys, values, out_cotangent, proj_weight):
    tok, width = queries.shape
    heads = width // DH
    ny, nz = lax.axis_size("y"), lax.axis_size("z")
    nx, nc = lax.axis_size("x"), lax.axis_size("c")
    cols = out_cotangent.shape[1]
    scale = (DH * tok * ny * nz) ** -0.5
    place = lax.axis_index("y").reshape(1)
    weight_t = proj_weight.T
    own = weight_t.shape[0]
    share = DH // nz
    square = 2 * tok * DH * DH * heads
    wide = 2 * tok * tok * DH * heads
    big = tok * width

    sent = local_call(
        first_kernel, shape((nz, own + share, width), BF16), square, 3 * big
    )(keys, values, weight_t)
    got = exchange(sent, "z")
    weight_z, kv_part, kv_total = local_call(
        split_kernel,
        (
            shape((nz * own, width), BF16),
            shape((nz, share, width), F32),
            shape((ny, share, width), F32),
        ),
        0,
        2 * big,
    )(got)
    weight_full = lax.all_gather(weight_z, "y", axis=0, tiled=True)
    cot_own, kv_total = lax.optimization_barrier((out_cotangent, kv_total))
    cot_c = lax.all_gather(cot_own, "c")
    cot_all = exchange(jnp.broadcast_to(cot_c[None], (nx,) + cot_c.shape), "x")
    attn, attn_inner = local_call(
        attn_kernel,
        (shape((heads, tok, tok), BF16), shape((tok, width), F32)),
        2 * wide,
        10 * big,
    )(queries, keys, values)
    prior = exchange(join(place, exchange(kv_total, "y"), kv_part, False), "z")
    prior = prior.reshape(DH, width)

    n_blocks = nx * nc
    cot_blocks = cot_all.reshape(n_blocks, tok, cols)

    whole = pl.BlockSpec((tok, width), lambda i: (0, 0))
    state = pl.BlockSpec((DH, width), lambda i: (0, 0))
    cot_spec = pl.BlockSpec((1, tok, cols), lambda i: (i, 0, 0))
    by_block = pl.BlockSpec((cols, width), lambda i: (i, 0))
    proj_term = local_call(
        functools.partial(proj_kernel, scale),
        shape((n_blocks * cols, width), F32),
        square + 2 * tok * cols * width * n_blocks,
        4 * n_blocks * cols * width,
        grid=(n_blocks,),
        in_specs=[whole, state, whole, cot_spec],
        out_specs=by_block,
        scratch_shapes=[pltpu.VMEM((tok, width), BF16)],
    )(queries, prior, attn_inner, cot_blocks)
    proj_y = lax.psum_scatter(proj_term, "y", scatter_dimension=0, tiled=True)

    grad_out, qg = local_call(
        grad_out_kernel,
        (shape((tok, width), BF16), shape((DH, width), BF16)),
        square + 2 * tok * cols * width * n_blocks,
        2 * n_blocks * cols * width,
        grid=(n_blocks,),
        in_specs=[cot_spec, by_block, whole],
        out_specs=[whole, state],
        scratch_shapes=[pltpu.VMEM((tok, width), F32)],
    )(cot_blocks, weight_full, queries)
    qg_got = exchange(qg.reshape(nz, share, width), "z")
    qg_part, qg_total = local_call(
        back_scan_kernel,
        (shape((nz, share, width), F32), shape((ny, share, width), F32)),
        0,
        2 * big,
    )(qg_got)
    grad_q, near_k, near_v = local_call(
        functools.partial(inner_grads_kernel, scale),
        (shape((tok, width), BF16), shape((tok, width), F32), shape((tok, width), F32)),
        4 * wide + square,
        16 * big,
    )(queries, keys, values, grad_out, attn, prior)
    later = exchange(join(place, exchange(qg_total, "y"), qg_part, True), "z")
    later = later.reshape(DH, width)
    grad_k, grad_v = local_call(
        functools.partial(outer_grads_kernel, scale),
        (shape((tok, width), BF16), shape((tok, width), BF16)),
        2 * square,
        12 * big,
    )(keys, values, later, near_k, near_v)

    proj_parts = exchange(proj_y.astype(BF16).reshape(nz, own, width), "z")
    proj_sum = jnp.sum(proj_parts.astype(F32), axis=0)
    grad_proj = (proj_sum / jnp.sqrt(F32(tok * ny * nz))).T
    return grad_q, grad_k, grad_v, grad_proj


def solution(mesh):
    seq, tp = mesh.devices.shape
    inner, cores = 8, 2
    grid = Mesh(
        mesh.devices.reshape(seq // inner, inner, tp // cores, cores), ("y", "z", "x", "c")
    )
    tokens, weight = P(SEQ, ("x", "c")), P(("x", "c"), SEQ)
    return jax.shard_map(
        per_device,
        mesh=grid,
        in_specs=(tokens, tokens, tokens, tokens, weight),
        out_specs=(tokens, tokens, tokens, weight),
        check_vma=False,
    )
```

```python
import functools

import jax
import jax.numpy as jnp
from jax import lax
from jax.experimental import pallas as pl
from jax.experimental.pallas import tpu as pltpu
from jax.sharding import Mesh, PartitionSpec as P

DH = 128
SEQ = ("y", "z")
BF16 = jnp.bfloat16
F32 = jnp.float32
VMEM_BYTES = 48 * 1024 * 1024


def mm(a, b, ca, cb):
    return lax.dot_general(a, b, (((ca,), (cb,)), ((), ())), preferred_element_type=F32)


def head(h):
    return slice(h * DH, (h + 1) * DH)


def local_call(kernel, out_shape, flops, moved, **kwargs):
    return pl.pallas_call(
        kernel,
        out_shape=out_shape,
        cost_estimate=pl.CostEstimate(flops=flops, transcendentals=0, bytes_accessed=moved),
        compiler_params=pltpu.CompilerParams(vmem_limit_bytes=VMEM_BYTES),
        **kwargs,
    )


def causal(tok):
    rows = lax.broadcasted_iota(jnp.int32, (tok, tok), 0)
    cols = lax.broadcasted_iota(jnp.int32, (tok, tok), 1)
    return rows >= cols


def exchange(x, axis):
    return lax.all_to_all(x, axis, 0, 0, tiled=True)


def first_kernel(k_ref, v_ref, w_ref, out_ref):
    peers, rows, width = out_ref.shape
    own = w_ref.shape[0]
    share = rows - own
    for h in range(width // DH):
        kv = mm(k_ref[:, head(h)], v_ref[:, head(h)], 0, 0).astype(BF16)
        for p in range(peers):
            out_ref[p, own:, head(h)] = kv[p * share : (p + 1) * share]
    for p in range(peers):
        out_ref[p, :own, :] = w_ref[...]


def split_kernel(got_ref, weight_ref, part_ref, total_ref):
    peers, rows, width = got_ref.shape
    own = weight_ref.shape[0] // peers
    running = jnp.zeros((rows - own, width), F32)
    for p in range(peers):
        weight_ref[p * own : (p + 1) * own, :] = got_ref[p, :own, :]
        part_ref[p] = running
        running = running + got_ref[p, own:, :].astype(F32)
    for p in range(total_ref.shape[0]):
        total_ref[p] = running


def back_scan_kernel(got_ref, part_ref, total_ref):
    peers, rows, width = got_ref.shape
    running = jnp.zeros((rows, width), F32)
    for p in reversed(range(peers)):
        part_ref[p] = running
        running = running + got_ref[p].astype(F32)
    for p in range(total_ref.shape[0]):
        total_ref[p] = running


def join_kernel(reverse, place_ref, totals_ref, part_ref, out_ref):
    place = place_ref[0]
    base = jnp.zeros(totals_ref.shape[1:], F32)
    for other in range(totals_ref.shape[0]):
        counts = place < other if reverse else place > other
        base = base + jnp.where(counts, totals_ref[other], 0.0)
    for p in range(part_ref.shape[0]):
        out_ref[p] = (base + part_ref[p]).astype(out_ref.dtype)


def attn_kernel(q_ref, k_ref, v_ref, attn_ref, inner_ref):
    mask = causal(q_ref.shape[0])
    for h in range(q_ref.shape[1] // DH):
        scores = mm(q_ref[:, head(h)], k_ref[:, head(h)], 1, 1)
        attn = jnp.where(mask, scores, 0.0).astype(BF16)
        attn_ref[h] = attn
        inner_ref[:, head(h)] = mm(attn, v_ref[:, head(h)], 1, 0)


def proj_kernel(scale, q_ref, prior_ref, inner_ref, top_ref, low_ref, out_ref, attn_out_ref):
    @pl.when(pl.program_id(0) == 0)
    def _():
        for h in range(q_ref.shape[1] // DH):
            far = mm(q_ref[:, head(h)], prior_ref[:, head(h)], 1, 0)
            attn_out_ref[:, head(h)] = (scale * (inner_ref[:, head(h)] + far)).astype(BF16)

    cot = jnp.concatenate([top_ref[0], low_ref[0]], axis=0)
    out_ref[...] = mm(cot, attn_out_ref[...], 0, 0)


def grad_out_kernel(top_ref, low_ref, w_ref, q_ref, g_ref, qg_ref, acc_ref):
    step = pl.program_id(0)
    cot = jnp.concatenate([top_ref[0], low_ref[0]], axis=0)
    term = mm(cot, w_ref[...], 1, 0)

    @pl.when(step == 0)
    def _():
        acc_ref[...] = term

    @pl.when(step > 0)
    def _():
        acc_ref[...] += term

    @pl.when(step == pl.num_programs(0) - 1)
    def _():
        g = acc_ref[...].astype(BF16)
        g_ref[...] = g
        for h in range(g.shape[1] // DH):
            qg_ref[:, head(h)] = mm(q_ref[:, head(h)], g[:, head(h)], 0, 0).astype(BF16)


def inner_grads_kernel(scale, q_ref, k_ref, v_ref, g_ref, attn_ref, prior_ref, dq_ref, dk_ref, dv_ref):
    mask = causal(q_ref.shape[0])
    for h in range(q_ref.shape[1] // DH):
        g = g_ref[:, head(h)]
        back = jnp.where(mask, mm(g, v_ref[:, head(h)], 1, 1), 0.0).astype(BF16)
        near = mm(back, k_ref[:, head(h)], 1, 0)
        far = mm(g, prior_ref[:, head(h)], 1, 1)
        dq_ref[:, head(h)] = (scale * (near + far)).astype(BF16)
        dk_ref[:, head(h)] = mm(back, q_ref[:, head(h)], 0, 0)
        dv_ref[:, head(h)] = mm(attn_ref[h], g, 0, 0)


def outer_grads_kernel(scale, k_ref, v_ref, later_ref, near_k_ref, near_v_ref, dk_ref, dv_ref):
    for h in range(k_ref.shape[1] // DH):
        later = later_ref[:, head(h)]
        far_k = mm(v_ref[:, head(h)], later, 1, 1)
        dk_ref[:, head(h)] = (scale * (near_k_ref[:, head(h)] + far_k)).astype(BF16)
        far_v = mm(k_ref[:, head(h)], later, 1, 0)
        dv_ref[:, head(h)] = (scale * (near_v_ref[:, head(h)] + far_v)).astype(BF16)


def shape(dims, dtype):
    return jax.ShapeDtypeStruct(dims, dtype)


def in_hbm(x):
    return pltpu.with_memory_space_constraint(x, pltpu.HBM)


def join(place, totals, part, reverse):
    return local_call(
        functools.partial(join_kernel, reverse),
        shape(part.shape, BF16),
        0,
        3 * part.size * 4,
        in_specs=[
            pl.BlockSpec(memory_space=pltpu.SMEM),
            pl.BlockSpec(memory_space=pltpu.VMEM),
            pl.BlockSpec(memory_space=pltpu.VMEM),
        ],
    )(place, totals, part)


def per_device(queries, keys, values, out_cotangent, proj_weight):
    tok, width = queries.shape
    heads = width // DH
    ny, nz = lax.axis_size("y"), lax.axis_size("z")
    nx, nc = lax.axis_size("x"), lax.axis_size("c")
    cols = out_cotangent.shape[1]
    scale = (DH * tok * ny * nz) ** -0.5
    place = lax.axis_index("y").reshape(1)
    weight_t = proj_weight.T
    own = weight_t.shape[0]
    share = DH // nz
    square = 2 * tok * DH * DH * heads
    wide = 2 * tok * tok * DH * heads
    big = tok * width

    sent = local_call(
        first_kernel, shape((nz, own + share, width), BF16), square, 3 * big
    )(in_hbm(keys), in_hbm(values), in_hbm(weight_t))
    got = exchange(sent, "z")
    weight_z, kv_part, kv_total = local_call(
        split_kernel,
        (
            shape((nz * own, width), BF16),
            shape((nz, share, width), F32),
            shape((ny, share, width), F32),
        ),
        0,
        2 * big,
    )(got)
    weight_full = lax.all_gather(weight_z, "y", axis=0, tiled=True)
    cot_own, kv_total = lax.optimization_barrier((out_cotangent, kv_total))
    cot_x = lax.all_gather(cot_own, "x")
    half = tok // 2
    cot_top = lax.all_gather(cot_x[:, :half], "c").reshape(nx * nc, half, cols)
    cot_low = lax.all_gather(cot_x[:, half:], "c").reshape(nx * nc, half, cols)
    attn, attn_inner = local_call(
        attn_kernel,
        (shape((heads, tok, tok), BF16), shape((tok, width), F32)),
        2 * wide,
        10 * big,
    )(queries, keys, values)
    prior = exchange(join(place, exchange(kv_total, "y"), kv_part, False), "z")
    prior = prior.reshape(DH, width)

    n_blocks = nx * nc

    def block_of(i):
        return (i % nx) * nc + i // nx

    whole = pl.BlockSpec((tok, width), lambda i: (0, 0))
    state = pl.BlockSpec((DH, width), lambda i: (0, 0))
    cot_spec = pl.BlockSpec((1, half, cols), lambda i: (i, 0, 0))
    by_block = pl.BlockSpec((cols, width), lambda i: (block_of(i), 0))
    proj_term = local_call(
        functools.partial(proj_kernel, scale),
        pltpu.HBM((n_blocks * cols, width), F32),
        square + 2 * tok * cols * width * n_blocks,
        4 * n_blocks * cols * width,
        grid=(n_blocks,),
        in_specs=[whole, state, whole, cot_spec, cot_spec],
        out_specs=by_block,
        scratch_shapes=[pltpu.VMEM((tok, width), BF16)],
    )(queries, prior, attn_inner, cot_top, cot_low)
    proj_y = lax.psum_scatter(proj_term, "y", scatter_dimension=0, tiled=True)

    grad_out, qg = local_call(
        grad_out_kernel,
        (shape((tok, width), BF16), shape((DH, width), BF16)),
        square + 2 * tok * cols * width * n_blocks,
        2 * n_blocks * cols * width,
        grid=(n_blocks,),
        in_specs=[cot_spec, cot_spec, by_block, whole],
        out_specs=[whole, state],
        scratch_shapes=[pltpu.VMEM((tok, width), F32)],
    )(cot_top, cot_low, in_hbm(weight_full), queries)
    qg_got = exchange(qg.reshape(nz, share, width), "z")
    qg_part, qg_total = local_call(
        back_scan_kernel,
        (shape((nz, share, width), F32), shape((ny, share, width), F32)),
        0,
        2 * big,
    )(qg_got)
    grad_q, near_k, near_v = local_call(
        functools.partial(inner_grads_kernel, scale),
        (shape((tok, width), BF16), shape((tok, width), F32), shape((tok, width), F32)),
        4 * wide + square,
        16 * big,
    )(queries, keys, values, grad_out, attn, prior)
    later = exchange(join(place, exchange(qg_total, "y"), qg_part, True), "z")
    later = later.reshape(DH, width)
    grad_k, grad_v = local_call(
        functools.partial(outer_grads_kernel, scale),
        (shape((tok, width), BF16), shape((tok, width), BF16)),
        2 * square,
        12 * big,
    )(keys, values, later, near_k, near_v)

    proj_parts = exchange(proj_y.astype(BF16).reshape(nz, own, width), "z")
    proj_sum = jnp.sum(proj_parts.astype(F32), axis=0)
    grad_proj = (proj_sum / jnp.sqrt(F32(tok * ny * nz))).T
    return grad_q, grad_k, grad_v, grad_proj


def solution(mesh):
    seq, tp = mesh.devices.shape
    inner, cores = 8, 2
    grid = Mesh(
        mesh.devices.reshape(seq // inner, inner, tp // cores, cores), ("y", "z", "x", "c")
    )
    tokens, weight = P(SEQ, ("x", "c")), P(("x", "c"), SEQ)
    return jax.shard_map(
        per_device,
        mesh=grid,
        in_specs=(tokens, tokens, tokens, tokens, weight),
        out_specs=(tokens, tokens, tokens, weight),
        check_vma=False,
    )
```

```python
import functools

import jax
import jax.numpy as jnp
from jax import lax
from jax.experimental import pallas as pl
from jax.experimental.pallas import tpu as pltpu
from jax.sharding import Mesh, PartitionSpec as P

DH = 128
SEQ = ("y", "z")
BF16 = jnp.bfloat16
F32 = jnp.float32
VMEM_BYTES = 48 * 1024 * 1024


def mm(a, b, ca, cb):
    return lax.dot_general(a, b, (((ca,), (cb,)), ((), ())), preferred_element_type=F32)


def head(h):
    return slice(h * DH, (h + 1) * DH)


def local_call(kernel, out_shape, flops, moved, **kwargs):
    return pl.pallas_call(
        kernel,
        out_shape=out_shape,
        cost_estimate=pl.CostEstimate(flops=flops, transcendentals=0, bytes_accessed=moved),
        compiler_params=pltpu.CompilerParams(vmem_limit_bytes=VMEM_BYTES),
        **kwargs,
    )


def causal(tok):
    rows = lax.broadcasted_iota(jnp.int32, (tok, tok), 0)
    cols = lax.broadcasted_iota(jnp.int32, (tok, tok), 1)
    return rows >= cols


def exchange(x, axis):
    return lax.all_to_all(x, axis, 0, 0, tiled=True)


def first_kernel(k_ref, v_ref, w_ref, out_ref):
    peers, rows, width = out_ref.shape
    own = w_ref.shape[0]
    share = (rows - own) // 2
    for h in range(width // DH):
        kv = mm(k_ref[:, head(h)], v_ref[:, head(h)], 0, 0)
        high = kv.astype(BF16)
        low = (kv - high.astype(F32)).astype(BF16)
        for p in range(peers):
            out_ref[p, own : own + share, head(h)] = high[p * share : (p + 1) * share]
            out_ref[p, own + share :, head(h)] = low[p * share : (p + 1) * share]
    for p in range(peers):
        out_ref[p, :own, :] = w_ref[...]


def split_kernel(got_ref, weight_ref, part_ref, total_ref):
    peers, rows, width = got_ref.shape
    own = weight_ref.shape[0] // peers
    share = (rows - own) // 2
    running = jnp.zeros((share, width), F32)
    for p in range(peers):
        weight_ref[p * own : (p + 1) * own, :] = got_ref[p, :own, :]
        part_ref[p] = running
        high = got_ref[p, own : own + share, :].astype(F32)
        running = running + (high + got_ref[p, own + share :, :].astype(F32))
    for p in range(total_ref.shape[0]):
        total_ref[p] = running


def back_scan_kernel(got_ref, part_ref, total_ref):
    peers, rows, width = got_ref.shape
    running = jnp.zeros((rows, width), F32)
    for p in reversed(range(peers)):
        part_ref[p] = running
        running = running + got_ref[p]
    for p in range(total_ref.shape[0]):
        total_ref[p] = running


def join_kernel(reverse, place_ref, totals_ref, part_ref, out_ref):
    place = place_ref[0]
    base = jnp.zeros(totals_ref.shape[1:], F32)
    for other in range(totals_ref.shape[0]):
        counts = place < other if reverse else place > other
        base = base + jnp.where(counts, totals_ref[other], 0.0)
    for p in range(part_ref.shape[0]):
        out_ref[p] = (base + part_ref[p]).astype(out_ref.dtype)


def attn_kernel(q_ref, k_ref, v_ref, attn_ref, inner_ref):
    mask = causal(q_ref.shape[0])
    for h in range(q_ref.shape[1] // DH):
        scores = mm(q_ref[:, head(h)], k_ref[:, head(h)], 1, 1)
        attn = jnp.where(mask, scores, 0.0).astype(BF16)
        attn_ref[h] = attn
        inner_ref[:, head(h)] = mm(attn, v_ref[:, head(h)], 1, 0)


def proj_kernel(scale, q_ref, prior_ref, inner_ref, top_ref, low_ref, out_ref, attn_out_ref):
    @pl.when(pl.program_id(0) == 0)
    def _():
        for h in range(q_ref.shape[1] // DH):
            far = mm(q_ref[:, head(h)], prior_ref[:, head(h)], 1, 0)
            attn_out_ref[:, head(h)] = (scale * (inner_ref[:, head(h)] + far)).astype(BF16)

    for x in range(out_ref.shape[0]):
        cot = jnp.concatenate([top_ref[0, x], low_ref[0, x]], axis=0)
        out_ref[x, 0] = mm(cot, attn_out_ref[...], 0, 0).astype(BF16)


def grad_out_kernel(top_ref, low_ref, w_ref, q_ref, g_ref, qg_ref, acc_ref):
    step = pl.program_id(0)
    term = None
    for x in range(w_ref.shape[0]):
        cot = jnp.concatenate([top_ref[0, x], low_ref[0, x]], axis=0)
        one = mm(cot, w_ref[x, 0], 1, 0)
        term = one if term is None else term + one

    @pl.when(step == 0)
    def _():
        acc_ref[...] = term

    @pl.when(step > 0)
    def _():
        acc_ref[...] += term

    @pl.when(step == pl.num_programs(0) - 1)
    def _():
        g = acc_ref[...].astype(BF16)
        g_ref[...] = g
        for h in range(g.shape[1] // DH):
            qg_ref[:, head(h)] = mm(q_ref[:, head(h)], g[:, head(h)], 0, 0)


def inner_grads_kernel(scale, q_ref, k_ref, v_ref, g_ref, attn_ref, prior_ref, dq_ref, dk_ref, dv_ref):
    mask = causal(q_ref.shape[0])
    for h in range(q_ref.shape[1] // DH):
        g = g_ref[:, head(h)]
        back = jnp.where(mask, mm(g, v_ref[:, head(h)], 1, 1), 0.0).astype(BF16)
        near = mm(back, k_ref[:, head(h)], 1, 0)
        far = mm(g, prior_ref[:, head(h)], 1, 1)
        dq_ref[:, head(h)] = (scale * (near + far)).astype(BF16)
        dk_ref[:, head(h)] = mm(back, q_ref[:, head(h)], 0, 0)
        dv_ref[:, head(h)] = mm(attn_ref[h], g, 0, 0)


def outer_grads_kernel(scale, k_ref, v_ref, later_ref, near_k_ref, near_v_ref, dk_ref, dv_ref):
    for h in range(k_ref.shape[1] // DH):
        later = later_ref[:, head(h)]
        far_k = mm(v_ref[:, head(h)], later, 1, 1)
        dk_ref[:, head(h)] = (scale * (near_k_ref[:, head(h)] + far_k)).astype(BF16)
        far_v = mm(k_ref[:, head(h)], later, 1, 0)
        dv_ref[:, head(h)] = (scale * (near_v_ref[:, head(h)] + far_v)).astype(BF16)


def shape(dims, dtype):
    return jax.ShapeDtypeStruct(dims, dtype)


def in_hbm(x):
    return pltpu.with_memory_space_constraint(x, pltpu.HBM)


def join(place, totals, part, reverse):
    return local_call(
        functools.partial(join_kernel, reverse),
        shape(part.shape, BF16),
        0,
        3 * part.size * 4,
        in_specs=[
            pl.BlockSpec(memory_space=pltpu.SMEM),
            pl.BlockSpec(memory_space=pltpu.VMEM),
            pl.BlockSpec(memory_space=pltpu.VMEM),
        ],
    )(place, totals, part)


def per_device(queries, keys, values, out_cotangent, proj_weight):
    tok, width = queries.shape
    heads = width // DH
    ny, nz = lax.axis_size("y"), lax.axis_size("z")
    nx, nc = lax.axis_size("x"), lax.axis_size("c")
    cols = out_cotangent.shape[1]
    scale = (DH * tok * ny * nz) ** -0.5
    place = lax.axis_index("y").reshape(1)
    weight_t = proj_weight.T
    own = weight_t.shape[0]
    share = DH // nz
    square = 2 * tok * DH * DH * heads
    wide = 2 * tok * tok * DH * heads
    big = tok * width

    sent = local_call(
        first_kernel, shape((nz, own + 2 * share, width), BF16), square, 3 * big
    )(in_hbm(keys), in_hbm(values), in_hbm(weight_t))
    got = exchange(sent, "z")
    weight_z, kv_part, kv_total = local_call(
        split_kernel,
        (
            shape((nz * own, width), BF16),
            shape((nz, share, width), F32),
            shape((ny, share, width), F32),
        ),
        0,
        2 * big,
    )(got)
    weight_full = lax.all_gather(weight_z, "y", axis=0, tiled=True)
    cot_own, kv_total = lax.optimization_barrier((out_cotangent, kv_total))
    cot_x = lax.all_gather(cot_own, "x")
    half = tok // 2
    cot_top = lax.all_gather(cot_x[:, :half], "c")
    cot_low = lax.all_gather(cot_x[:, half:], "c")
    attn, attn_inner = local_call(
        attn_kernel,
        (shape((heads, tok, tok), BF16), shape((tok, width), F32)),
        2 * wide,
        10 * big,
    )(queries, keys, values)
    prior = exchange(join(place, exchange(kv_total, "y"), kv_part, False), "z")
    prior = prior.reshape(DH, width)

    n_blocks = nx * nc

    whole = pl.BlockSpec((tok, width), lambda i: (0, 0))
    state = pl.BlockSpec((DH, width), lambda i: (0, 0))
    cot_spec = pl.BlockSpec((1, nx, half, cols), lambda i: (i, 0, 0, 0))
    by_core = pl.BlockSpec((nx, 1, cols, width), lambda i: (0, i, 0, 0))
    proj_term = local_call(
        functools.partial(proj_kernel, scale),
        pltpu.HBM((nx, nc, cols, width), BF16),
        square + 2 * tok * cols * width * n_blocks,
        2 * n_blocks * cols * width,
        grid=(nc,),
        in_specs=[whole, state, whole, cot_spec, cot_spec],
        out_specs=by_core,
        scratch_shapes=[pltpu.VMEM((tok, width), BF16)],
    )(queries, prior, attn_inner, cot_top, cot_low)
    proj_term = proj_term.reshape(n_blocks * cols, width)
    proj_y = lax.psum_scatter(proj_term, "y", scatter_dimension=0, tiled=True)

    grad_out, qg = local_call(
        grad_out_kernel,
        (shape((tok, width), BF16), shape((DH, width), F32)),
        square + 2 * tok * cols * width * n_blocks,
        2 * n_blocks * cols * width,
        grid=(nc,),
        in_specs=[cot_spec, cot_spec, by_core, whole],
        out_specs=[whole, state],
        scratch_shapes=[pltpu.VMEM((tok, width), F32)],
    )(cot_top, cot_low, in_hbm(weight_full.reshape(nx, nc, cols, width)), queries)
    qg_got = exchange(qg.reshape(nz, share, width), "z")
    qg_part, qg_total = local_call(
        back_scan_kernel,
        (shape((nz, share, width), F32), shape((ny, share, width), F32)),
        0,
        2 * big,
    )(qg_got)
    grad_q, near_k, near_v = local_call(
        functools.partial(inner_grads_kernel, scale),
        (shape((tok, width), BF16), shape((tok, width), F32), shape((tok, width), F32)),
        4 * wide + square,
        16 * big,
    )(queries, keys, values, grad_out, attn, prior)
    later = exchange(join(place, exchange(qg_total, "y"), qg_part, True), "z")
    later = later.reshape(DH, width)
    grad_k, grad_v = local_call(
        functools.partial(outer_grads_kernel, scale),
        (shape((tok, width), BF16), shape((tok, width), BF16)),
        2 * square,
        12 * big,
    )(keys, values, later, near_k, near_v)

    proj_parts = exchange(proj_y.reshape(nz, own, width), "z")
    proj_sum = jnp.sum(proj_parts.astype(F32), axis=0)
    grad_proj = (proj_sum / jnp.sqrt(F32(tok * ny * nz))).T
    return grad_q, grad_k, grad_v, grad_proj


def solution(mesh):
    seq, tp = mesh.devices.shape
    inner, cores = 8, 2
    grid = Mesh(
        mesh.devices.reshape(seq // inner, inner, tp // cores, cores), ("y", "z", "x", "c")
    )
    tokens, weight = P(SEQ, ("x", "c")), P(("x", "c"), SEQ)
    return jax.shard_map(
        per_device,
        mesh=grid,
        in_specs=(tokens, tokens, tokens, tokens, weight),
        out_specs=(tokens, tokens, tokens, weight),
        check_vma=False,
    )
```

```python
import functools

import jax
import jax.numpy as jnp
from jax import lax
from jax.experimental import pallas as pl
from jax.experimental.pallas import tpu as pltpu
from jax.sharding import Mesh, PartitionSpec as P

DH = 128
PAIR = "zl"
Z = ("zh", PAIR)
SEQ = ("y",) + Z
TP = ("x", "c")
BF16 = jnp.bfloat16
F32 = jnp.float32
VMEM_BYTES = 48 * 1024 * 1024
IN_VMEM = pl.BlockSpec(memory_space=pltpu.VMEM)
IN_SMEM = pl.BlockSpec(memory_space=pltpu.SMEM)


def mm(a, b, ca, cb):
    return lax.dot_general(a, b, (((ca,), (cb,)), ((), ())), preferred_element_type=F32)


def head(h):
    return slice(h * DH, (h + 1) * DH)


def local_call(kernel, out_shape, flops, moved, **kwargs):
    return pl.pallas_call(
        kernel,
        out_shape=out_shape,
        cost_estimate=pl.CostEstimate(flops=flops, transcendentals=0, bytes_accessed=moved),
        compiler_params=pltpu.CompilerParams(vmem_limit_bytes=VMEM_BYTES),
        **kwargs,
    )


def causal(tok):
    rows = lax.broadcasted_iota(jnp.int32, (tok, tok), 0)
    cols = lax.broadcasted_iota(jnp.int32, (tok, tok), 1)
    return rows >= cols


def exchange(x, axis):
    return lax.all_to_all(x, axis, 0, 0, tiled=True)


def first_kernel(k_ref, v_ref, w_ref, out_ref):
    count, rows, half = out_ref.shape
    own = w_ref.shape[0]
    share = rows - own
    per_head = DH // share
    for h in range(k_ref.shape[1] // DH):
        kv = mm(k_ref[:, head(h)], v_ref[:, head(h)], 0, 0)
        high = kv.astype(BF16)
        low = (kv - high.astype(F32)).astype(BF16)
        for i in range(per_head):
            piece = slice(i * share, (i + 1) * share)
            out_ref[h * per_head + i, own:, :DH] = high[piece]
            out_ref[h * per_head + i, own:, DH:] = low[piece]
    for s in range(count):
        out_ref[s, :own, :] = w_ref[:, (s % 2) * half : (s % 2 + 1) * half]


def prior_kernel(got_ref, sums_ref):
    count, share, _ = sums_ref.shape
    own = got_ref.shape[1] - share
    running = jnp.zeros(sums_ref.shape[1:], F32)
    for s in range(count):
        sums_ref[s] = running.astype(BF16)
        high = got_ref[s, own:, :DH].astype(F32)
        running = running + (high + got_ref[s, own:, DH:].astype(F32))


def later_kernel(got_ref, sums_ref):
    running = jnp.zeros(sums_ref.shape[1:], F32)
    for s in reversed(range(sums_ref.shape[0])):
        sums_ref[s] = running.astype(BF16)
        running = running + got_ref[s].astype(F32)


def attn_kernel(q_ref, k_ref, v_ref, attn_ref, inner_ref):
    mask = causal(q_ref.shape[0])
    for h in range(q_ref.shape[1] // DH):
        scores = mm(q_ref[:, head(h)], k_ref[:, head(h)], 1, 1)
        attn = jnp.where(mask, scores, 0.0).astype(BF16)
        attn_ref[h] = attn
        inner_ref[:, head(h)] = mm(attn, v_ref[:, head(h)], 1, 0)


def half_grad_kernel(place_ref, cot_ref, got_ref, keep_ref, send_ref):
    blocks, _, cols = cot_ref.shape[1:]
    own = cols * blocks // got_ref.shape[0]
    per_block = cols // own
    total = None
    for b in range(blocks):
        weight = got_ref[b * per_block : (b + 1) * per_block, :own, :]
        term = mm(cot_ref[0, b], weight.reshape(cols, weight.shape[2]), 1, 0)
        total = term if total is None else total + term
    mine = place_ref[0] == pl.program_id(0)

    @pl.when(mine)
    def _():
        keep_ref[...] = total.astype(BF16)

    @pl.when(jnp.logical_not(mine))
    def _():
        send_ref[...] = total.astype(BF16)


def proj_kernel(scale, place_ref, q_ref, prior_ref, inner_ref, cot_ref, out_ref, attn_out_ref):
    @pl.when(pl.program_id(0) == 0)
    def _():
        for h in range(q_ref.shape[1] // DH):
            far = mm(q_ref[:, head(h)], prior_ref[head(h), :], 1, 0)
            attn_out_ref[:, head(h)] = (scale * (inner_ref[:, head(h)] + far)).astype(BF16)

    for b in range(out_ref.shape[0]):
        out_ref[b] = mm(cot_ref[0, b], attn_out_ref[...], 0, 0).astype(BF16)


def qg_kernel(place_ref, keep_ref, got_ref, q_ref, g_ref, qg_ref):
    half = keep_ref.shape[1]
    first = place_ref[0] == 0
    g_ref[:, :half] = jnp.where(first, keep_ref[...], got_ref[...])
    g_ref[:, half:] = jnp.where(first, got_ref[...], keep_ref[...])
    for h in range(q_ref.shape[1] // DH):
        qg_ref[head(h), :] = mm(q_ref[:, head(h)], g_ref[:, head(h)], 0, 0).astype(BF16)


def inner_grads_kernel(scale, q_ref, k_ref, v_ref, g_ref, attn_ref, prior_ref, dq_ref, dk_ref, dv_ref):
    mask = causal(q_ref.shape[0])
    for h in range(q_ref.shape[1] // DH):
        g = g_ref[:, head(h)]
        back = jnp.where(mask, mm(g, v_ref[:, head(h)], 1, 1), 0.0).astype(BF16)
        near = mm(back, k_ref[:, head(h)], 1, 0)
        far = mm(g, prior_ref[head(h), :], 1, 1)
        dq_ref[:, head(h)] = (scale * (near + far)).astype(BF16)
        dk_ref[:, head(h)] = mm(back, q_ref[:, head(h)], 0, 0)
        dv_ref[:, head(h)] = mm(attn_ref[h], g, 0, 0)


def outer_grads_kernel(scale, k_ref, v_ref, later_ref, near_k_ref, near_v_ref, dk_ref, dv_ref):
    for h in range(k_ref.shape[1] // DH):
        later = later_ref[head(h), :]
        far_k = mm(v_ref[:, head(h)], later, 1, 1)
        dk_ref[:, head(h)] = (scale * (near_k_ref[:, head(h)] + far_k)).astype(BF16)
        far_v = mm(k_ref[:, head(h)], later, 1, 0)
        dv_ref[:, head(h)] = (scale * (near_v_ref[:, head(h)] + far_v)).astype(BF16)


def shape(dims, dtype):
    return jax.ShapeDtypeStruct(dims, dtype)


def in_hbm(x):
    return pltpu.with_memory_space_constraint(x, pltpu.HBM)


def per_device(queries, keys, values, out_cotangent, proj_weight):
    tok, width = queries.shape
    heads = width // DH
    count, nz, ny = lax.axis_size(SEQ), lax.axis_size(Z), lax.axis_size("y")
    blocks = lax.axis_size(TP)
    cols = out_cotangent.shape[1]
    scale = (DH * tok * count) ** -0.5
    place = lax.axis_index(PAIR).reshape(1)
    weight_t = proj_weight.T
    own = weight_t.shape[0]
    half = width // 2
    share = heads * DH // count
    square = 2 * tok * DH * DH * heads
    wide = 2 * tok * tok * DH * heads
    full = 2 * tok * cols * width * blocks
    big = tok * width

    sent = local_call(
        first_kernel, shape((count, own + share, half), BF16), square, 12 * big
    )(in_hbm(keys), in_hbm(values), in_hbm(weight_t))
    cot = lax.all_gather(out_cotangent, (PAIR,) + TP).reshape(2, blocks, tok, cols)
    got = exchange(sent, SEQ)
    attn, attn_inner = local_call(
        attn_kernel,
        (shape((heads, tok, tok), BF16), shape((tok, width), F32)),
        2 * wide,
        10 * big,
    )(queries, keys, values)
    sums = local_call(prior_kernel, shape((count, share, DH), BF16), 0, 4 * big)(got)
    prior = exchange(sums, SEQ).reshape(heads * DH, DH)

    keep, send = local_call(
        half_grad_kernel,
        (shape((tok, half), BF16), shape((tok, half), BF16)),
        full,
        24 * big,
        grid=(2,),
        in_specs=[
            IN_SMEM,
            pl.BlockSpec((1, blocks, tok, cols), lambda m: (m, 0, 0, 0)),
            pl.BlockSpec(got.shape, lambda m: (0, 0, 0)),
        ],
        out_specs=[pl.BlockSpec((tok, half), lambda m: (0, 0))] * 2,
    )(place, in_hbm(cot), got)
    swapped = lax.ppermute(send, PAIR, [(0, 1), (1, 0)])

    step = blocks // 2
    whole = pl.BlockSpec((tok, width), lambda i, p: (0, 0))
    proj_term = local_call(
        functools.partial(proj_kernel, scale),
        pltpu.HBM((blocks, cols, width), BF16),
        square + full,
        24 * big,
        grid_spec=pltpu.PrefetchScalarGridSpec(
            num_scalar_prefetch=1,
            grid=(blocks // step,),
            in_specs=[
                whole,
                pl.BlockSpec((heads * DH, DH), lambda i, p: (0, 0)),
                whole,
                pl.BlockSpec((1, step, tok, cols), lambda i, p: (p[0], i, 0, 0)),
            ],
            out_specs=pl.BlockSpec((step, cols, width), lambda i, p: (i, 0, 0)),
            scratch_shapes=[pltpu.VMEM((tok, width), BF16)],
        ),
    )(place, queries, prior, attn_inner, in_hbm(cot))
    proj_y = lax.psum_scatter(
        proj_term.reshape(blocks * cols, width), "y", scatter_dimension=0, tiled=True
    )

    grad_out, qg = local_call(
        qg_kernel,
        (shape((tok, width), BF16), shape((heads * DH, DH), BF16)),
        square,
        6 * big,
        in_specs=[IN_SMEM, IN_VMEM, IN_VMEM, IN_VMEM],
    )(place, keep, swapped, queries)
    qg_got = exchange(qg.reshape(count, share, DH), SEQ)
    sums = local_call(later_kernel, shape((count, share, DH), BF16), 0, 2 * big)(qg_got)
    later = exchange(sums, SEQ).reshape(heads * DH, DH)
    grad_q, near_k, near_v = local_call(
        functools.partial(inner_grads_kernel, scale),
        (shape((tok, width), BF16), shape((tok, width), F32), shape((tok, width), F32)),
        4 * wide + square,
        16 * big,
    )(queries, keys, values, grad_out, attn, prior)
    grad_k, grad_v = local_call(
        functools.partial(outer_grads_kernel, scale),
        (shape((tok, width), BF16), shape((tok, width), BF16)),
        2 * square,
        12 * big,
    )(keys, values, later, near_k, near_v)

    proj_parts = exchange(proj_y.reshape(nz, own, width), Z)
    proj_sum = jnp.sum(proj_parts.astype(F32), axis=0)
    grad_proj = (proj_sum / jnp.sqrt(F32(tok * count))).T
    return grad_q, grad_k, grad_v, grad_proj


def solution(mesh):
    seq, tp = mesh.devices.shape
    inner, cores = 8, 2
    grid = Mesh(
        mesh.devices.reshape(seq // inner, inner // 2, 2, tp // cores, cores),
        ("y", "zh", PAIR, "x", "c"),
    )
    tokens, weight = P(SEQ, TP), P(TP, SEQ)
    return jax.shard_map(
        per_device,
        mesh=grid,
        in_specs=(tokens, tokens, tokens, tokens, weight),
        out_specs=(tokens, tokens, tokens, weight),
        check_vma=False,
    )
```

```python
import functools

import jax
import jax.numpy as jnp
from jax import lax
from jax.experimental import pallas as pl
from jax.experimental.pallas import tpu as pltpu
from jax.sharding import Mesh, PartitionSpec as P

DH = 128
PAIR = "zl"
Z = ("zh", PAIR)
SEQ = ("y",) + Z
TP = ("x", "c")
BF16 = jnp.bfloat16
F32 = jnp.float32
VMEM_BYTES = 24 * 1024 * 1024
IN_VMEM = pl.BlockSpec(memory_space=pltpu.VMEM)
IN_SMEM = pl.BlockSpec(memory_space=pltpu.SMEM)


def mm(a, b, ca, cb):
    return lax.dot_general(a, b, (((ca,), (cb,)), ((), ())), preferred_element_type=F32)


def head(h):
    return slice(h * DH, (h + 1) * DH)


def local_call(kernel, out_shape, flops, moved, **kwargs):
    return pl.pallas_call(
        kernel,
        out_shape=out_shape,
        cost_estimate=pl.CostEstimate(flops=flops, transcendentals=0, bytes_accessed=moved),
        compiler_params=pltpu.CompilerParams(vmem_limit_bytes=VMEM_BYTES),
        **kwargs,
    )


def causal(tok):
    rows = lax.broadcasted_iota(jnp.int32, (tok, tok), 0)
    cols = lax.broadcasted_iota(jnp.int32, (tok, tok), 1)
    return rows >= cols


def exchange(x, axis):
    return lax.all_to_all(x, axis, 0, 0, tiled=True)


def first_kernel(k_ref, v_ref, w_ref, out_ref):
    count, rows, _ = out_ref.shape
    own = w_ref.shape[0]
    share = (rows - 2 * own) // 2
    per_head = DH // share
    for h in range(k_ref.shape[1] // DH):
        kv = mm(k_ref[:, head(h)], v_ref[:, head(h)], 0, 0)
        high = kv.astype(BF16)
        low = (kv - high.astype(F32)).astype(BF16)
        for i in range(per_head):
            piece = slice(i * share, (i + 1) * share)
            out_ref[h * per_head + i, 2 * own : 2 * own + share, :] = high[piece]
            out_ref[h * per_head + i, 2 * own + share :, :] = low[piece]
    for s in range(count):
        out_ref[s, :own, :] = w_ref[:, head(2 * (s % 2))]
        out_ref[s, own : 2 * own, :] = w_ref[:, head(2 * (s % 2) + 1)]


def prior_kernel(got_ref, sums_ref):
    count, share, _ = sums_ref.shape
    at = got_ref.shape[1] - 2 * share
    running = jnp.zeros(sums_ref.shape[1:], F32)
    for s in range(count):
        sums_ref[s] = running.astype(BF16)
        high = got_ref[s, at : at + share, :].astype(F32)
        running = running + (high + got_ref[s, at + share :, :].astype(F32))


def later_kernel(got_ref, sums_ref):
    running = jnp.zeros(sums_ref.shape[1:], F32)
    for s in reversed(range(sums_ref.shape[0])):
        sums_ref[s] = running.astype(BF16)
        running = running + got_ref[s].astype(F32)


def attn_kernel(q_ref, k_ref, v_ref, attn_ref, inner_ref):
    mask = causal(q_ref.shape[0])
    for h in range(q_ref.shape[1] // DH):
        scores = mm(q_ref[:, head(h)], k_ref[:, head(h)], 1, 1)
        attn = jnp.where(mask, scores, 0.0).astype(BF16)
        attn_ref[h] = attn
        inner_ref[:, head(h)] = mm(attn, v_ref[:, head(h)], 1, 0)


def half_grad_kernel(own, top_ref, low_ref, other_top_ref, other_low_ref, got_ref, keep_ref, send_ref):
    cores, chips, _, cols = top_ref.shape
    per_block = cols // own
    kept, sent = None, None
    for x in range(chips):
        for c in range(cores):
            b = x * cores + c
            sources = slice(b * per_block, (b + 1) * per_block)
            left = got_ref[sources, :own, :].reshape(cols, DH)
            right = got_ref[sources, own : 2 * own, :].reshape(cols, DH)
            weight = jnp.concatenate([left, right], axis=1)
            cot = jnp.concatenate([top_ref[c, x], low_ref[c, x]], axis=0)
            term = mm(cot, weight, 1, 0)
            kept = term if kept is None else kept + term
            cot = jnp.concatenate([other_top_ref[c, x], other_low_ref[c, x]], axis=0)
            term = mm(cot, weight, 1, 0)
            sent = term if sent is None else sent + term
    keep_ref[...] = kept.astype(BF16)
    send_ref[...] = sent.astype(BF16)


def proj_kernel(scale, q_ref, prior_ref, inner_ref, top_ref, low_ref, out_ref, attn_out_ref):
    @pl.when(pl.program_id(0) == 0)
    def _():
        for h in range(q_ref.shape[1] // DH):
            far = mm(q_ref[:, head(h)], prior_ref[head(h), :], 1, 0)
            attn_out_ref[:, head(h)] = (scale * (inner_ref[:, head(h)] + far)).astype(BF16)

    for x in range(out_ref.shape[0]):
        cot = jnp.concatenate([top_ref[0, x], low_ref[0, x]], axis=0)
        out_ref[x, 0] = mm(cot, attn_out_ref[...], 0, 0).astype(BF16)


def qg_kernel(place_ref, keep_ref, got_ref, q_ref, g_ref, qg_ref):
    half = keep_ref.shape[1]
    first = place_ref[0] == 0
    g_ref[:, :half] = jnp.where(first, keep_ref[...], got_ref[...])
    g_ref[:, half:] = jnp.where(first, got_ref[...], keep_ref[...])
    for h in range(q_ref.shape[1] // DH):
        qg_ref[head(h), :] = mm(q_ref[:, head(h)], g_ref[:, head(h)], 0, 0).astype(BF16)


def inner_grads_kernel(scale, q_ref, k_ref, v_ref, g_ref, attn_ref, prior_ref, dq_ref, dk_ref, dv_ref):
    mask = causal(q_ref.shape[0])
    for h in range(q_ref.shape[1] // DH):
        g = g_ref[:, head(h)]
        back = jnp.where(mask, mm(g, v_ref[:, head(h)], 1, 1), 0.0).astype(BF16)
        near = mm(back, k_ref[:, head(h)], 1, 0)
        far = mm(g, prior_ref[head(h), :], 1, 1)
        dq_ref[:, head(h)] = (scale * (near + far)).astype(BF16)
        dk_ref[:, head(h)] = mm(back, q_ref[:, head(h)], 0, 0)
        dv_ref[:, head(h)] = mm(attn_ref[h], g, 0, 0)


def outer_grads_kernel(scale, k_ref, v_ref, later_ref, near_k_ref, near_v_ref, dk_ref, dv_ref):
    for h in range(k_ref.shape[1] // DH):
        later = later_ref[head(h), :]
        far_k = mm(v_ref[:, head(h)], later, 1, 1)
        dk_ref[:, head(h)] = (scale * (near_k_ref[:, head(h)] + far_k)).astype(BF16)
        far_v = mm(k_ref[:, head(h)], later, 1, 0)
        dv_ref[:, head(h)] = (scale * (near_v_ref[:, head(h)] + far_v)).astype(BF16)


def shape(dims, dtype):
    return jax.ShapeDtypeStruct(dims, dtype)


def in_hbm(x):
    return pltpu.with_memory_space_constraint(x, pltpu.HBM)


def per_device(queries, keys, values, out_cotangent, proj_weight):
    tok, width = queries.shape
    heads = width // DH
    count, nz, ny = lax.axis_size(SEQ), lax.axis_size(Z), lax.axis_size("y")
    nx, nc = lax.axis_size("x"), lax.axis_size("c")
    blocks = nx * nc
    cols = out_cotangent.shape[1]
    scale = (DH * tok * count) ** -0.5
    place = lax.axis_index(PAIR).reshape(1)
    weight_t = proj_weight.T
    own = weight_t.shape[0]
    half = width // 2
    share = heads * DH // count
    square = 2 * tok * DH * DH * heads
    wide = 2 * tok * tok * DH * heads
    full = 2 * tok * cols * width * blocks
    big = tok * width

    sent = local_call(
        first_kernel, shape((count, 2 * own + 2 * share, DH), BF16), square, 12 * big
    )(in_hbm(keys), in_hbm(values), in_hbm(weight_t))
    cot_own, sent = lax.optimization_barrier((out_cotangent, sent))
    cot_other = lax.ppermute(cot_own, PAIR, [(0, 1), (1, 0)])
    got = exchange(sent, SEQ)

    own_x, other_x = lax.all_gather(cot_own, "x"), lax.all_gather(cot_other, "x")
    got, own_x, other_x = lax.optimization_barrier((got, own_x, other_x))
    rows = tok // 2
    own_top = lax.all_gather(own_x[:, :rows], "c")
    own_low = lax.all_gather(own_x[:, rows:], "c")
    other_top = lax.all_gather(other_x[:, :rows], "c")
    other_low = lax.all_gather(other_x[:, rows:], "c")
    attn, attn_inner = local_call(
        attn_kernel,
        (shape((heads, tok, tok), BF16), shape((tok, width), F32)),
        2 * wide,
        10 * big,
    )(queries, keys, values)
    sums = local_call(prior_kernel, shape((count, share, DH), BF16), 0, 4 * big)(got)
    prior = exchange(sums, SEQ).reshape(heads * DH, DH)

    keep, send = local_call(
        functools.partial(half_grad_kernel, own),
        (shape((tok, half), BF16), shape((tok, half), BF16)),
        full,
        24 * big,
    )(own_top, own_low, other_top, other_low, got)
    prior, keep, send = lax.optimization_barrier((prior, keep, send))
    swapped = lax.ppermute(send, PAIR, [(0, 1), (1, 0)])

    whole = pl.BlockSpec((tok, width), lambda i: (0, 0))
    cot_spec = pl.BlockSpec((1, nx, tok // 2, cols), lambda i: (i, 0, 0, 0))
    proj_term = local_call(
        functools.partial(proj_kernel, scale),
        pltpu.HBM((nx, nc, cols, width), BF16),
        square + full,
        24 * big,
        grid=(nc,),
        in_specs=[
            whole,
            pl.BlockSpec((heads * DH, DH), lambda i: (0, 0)),
            whole,
            cot_spec,
            cot_spec,
        ],
        out_specs=pl.BlockSpec((nx, 1, cols, width), lambda i: (0, i, 0, 0)),
        scratch_shapes=[pltpu.VMEM((tok, width), BF16)],
    )(queries, prior, attn_inner, own_top, own_low)
    proj_y = lax.psum_scatter(
        proj_term.reshape(blocks * cols, width), "y", scatter_dimension=0, tiled=True
    )

    grad_out, qg = local_call(
        qg_kernel,
        (shape((tok, width), BF16), shape((heads * DH, DH), BF16)),
        square,
        6 * big,
        in_specs=[IN_SMEM, IN_VMEM, IN_VMEM, IN_VMEM],
    )(place, keep, swapped, queries)
    qg_got = exchange(qg.reshape(count, share, DH), SEQ)
    sums = local_call(later_kernel, shape((count, share, DH), BF16), 0, 2 * big)(qg_got)
    later = exchange(sums, SEQ).reshape(heads * DH, DH)
    grad_q, near_k, near_v = local_call(
        functools.partial(inner_grads_kernel, scale),
        (shape((tok, width), BF16), shape((tok, width), F32), shape((tok, width), F32)),
        4 * wide + square,
        16 * big,
    )(queries, keys, values, grad_out, attn, prior)
    grad_k, grad_v = local_call(
        functools.partial(outer_grads_kernel, scale),
        (shape((tok, width), BF16), shape((tok, width), BF16)),
        2 * square,
        12 * big,
    )(keys, values, later, near_k, near_v)

    proj_parts = exchange(proj_y.reshape(nz, own, width), Z)
    proj_sum = jnp.sum(proj_parts.astype(F32), axis=0)
    grad_proj = (proj_sum / jnp.sqrt(F32(tok * count))).T
    return grad_q, grad_k, grad_v, grad_proj


def solution(mesh):
    seq, tp = mesh.devices.shape
    inner, cores = 8, 2
    grid = Mesh(
        mesh.devices.reshape(seq // inner, inner // 2, 2, tp // cores, cores),
        ("y", "zh", PAIR, "x", "c"),
    )
    tokens, weight = P(SEQ, TP), P(TP, SEQ)
    return jax.shard_map(
        per_device,
        mesh=grid,
        in_specs=(tokens, tokens, tokens, tokens, weight),
        out_specs=(tokens, tokens, tokens, weight),
        check_vma=False,
    )
```

```python
import functools

import jax
import jax.numpy as jnp
from jax import lax
from jax.experimental import pallas as pl
from jax.experimental.pallas import tpu as pltpu
from jax.sharding import Mesh, PartitionSpec as P

DH = 128
SEQ = ("y", "z")
BF16 = jnp.bfloat16
F32 = jnp.float32
VMEM_BYTES = 24 * 1024 * 1024


def mm(a, b, ca, cb):
    return lax.dot_general(a, b, (((ca,), (cb,)), ((), ())), preferred_element_type=F32)


def head(h):
    return slice(h * DH, (h + 1) * DH)


def local_call(kernel, out_shape, flops, moved, **kwargs):
    return pl.pallas_call(
        kernel,
        out_shape=out_shape,
        cost_estimate=pl.CostEstimate(flops=flops, transcendentals=0, bytes_accessed=moved),
        compiler_params=pltpu.CompilerParams(vmem_limit_bytes=VMEM_BYTES),
        **kwargs,
    )


def causal(tok):
    rows = lax.broadcasted_iota(jnp.int32, (tok, tok), 0)
    cols = lax.broadcasted_iota(jnp.int32, (tok, tok), 1)
    return rows >= cols


def exchange(x, axis):
    return lax.all_to_all(x, axis, 0, 0, tiled=True)


def first_kernel(k_ref, v_ref, w_ref, out_ref):
    peers, rows, width = out_ref.shape
    own = w_ref.shape[0]
    share = rows - own
    for h in range(width // DH):
        kv = mm(k_ref[:, head(h)], v_ref[:, head(h)], 0, 0).astype(BF16)
        for p in range(peers):
            out_ref[p, own:, head(h)] = kv[p * share : (p + 1) * share]
    for p in range(peers):
        out_ref[p, :own, :] = w_ref[...]


def split_kernel(got_ref, weight_ref, part_ref, total_ref):
    peers, rows, width = got_ref.shape
    own = weight_ref.shape[0] // peers
    running = jnp.zeros((rows - own, width), F32)
    for p in range(peers):
        weight_ref[p * own : (p + 1) * own, :] = got_ref[p, :own, :]
        part_ref[p] = running
        running = running + got_ref[p, own:, :].astype(F32)
    for p in range(total_ref.shape[0]):
        total_ref[p] = running


def later_kernel(got_ref, sums_ref):
    running = jnp.zeros(sums_ref.shape[1:], F32)
    for s in reversed(range(sums_ref.shape[0])):
        sums_ref[s] = running.astype(BF16)
        running = running + got_ref[s].astype(F32)


def join_kernel(place_ref, totals_ref, part_ref, out_ref):
    place = place_ref[0]
    base = jnp.zeros(totals_ref.shape[1:], F32)
    for other in range(totals_ref.shape[0]):
        counts = place > other
        base = base + jnp.where(counts, totals_ref[other], 0.0)
    for p in range(part_ref.shape[0]):
        out_ref[p] = (base + part_ref[p]).astype(out_ref.dtype)


def attn_kernel(q_ref, k_ref, v_ref, attn_ref, inner_ref):
    mask = causal(q_ref.shape[0])
    for h in range(q_ref.shape[1] // DH):
        scores = mm(q_ref[:, head(h)], k_ref[:, head(h)], 1, 1)
        attn = jnp.where(mask, scores, 0.0).astype(BF16)
        attn_ref[h] = attn
        inner_ref[:, head(h)] = mm(attn, v_ref[:, head(h)], 1, 0)


def attn_out_kernel(scale, q_ref, prior_ref, inner_ref, out_ref):
    for h in range(q_ref.shape[1] // DH):
        far = mm(q_ref[:, head(h)], prior_ref[:, head(h)], 1, 0)
        out_ref[:, head(h)] = (scale * (inner_ref[:, head(h)] + far)).astype(BF16)


def proj_kernel(attn_out_ref, top_ref, low_ref, out_ref, acc_ref):
    step = pl.program_id(0)
    total = None
    for x in range(attn_out_ref.shape[0]):
        cot = jnp.concatenate([top_ref[0, x], low_ref[0, x]], axis=0)
        term = mm(cot, attn_out_ref[x, 0], 0, 0)
        total = term if total is None else total + term

    @pl.when(step == 0)
    def _():
        acc_ref[...] = total

    @pl.when(step > 0)
    def _():
        acc_ref[...] += total

    @pl.when(step == pl.num_programs(0) - 1)
    def _():
        out_ref[...] = acc_ref[...].astype(BF16)


def grad_out_kernel(top_ref, low_ref, w_ref, q_ref, g_ref, qg_ref, acc_ref):
    step = pl.program_id(0)
    term = None
    for x in range(w_ref.shape[0]):
        cot = jnp.concatenate([top_ref[0, x], low_ref[0, x]], axis=0)
        one = mm(cot, w_ref[x, 0], 1, 0)
        term = one if term is None else term + one

    @pl.when(step == 0)
    def _():
        acc_ref[...] = term

    @pl.when(step > 0)
    def _():
        acc_ref[...] += term

    @pl.when(step == pl.num_programs(0) - 1)
    def _():
        g = acc_ref[...].astype(BF16)
        g_ref[...] = g
        for h in range(g.shape[1] // DH):
            qg_ref[head(h), :] = mm(q_ref[:, head(h)], g[:, head(h)], 0, 0).astype(BF16)


def inner_grads_kernel(scale, q_ref, k_ref, v_ref, g_ref, attn_ref, prior_ref, dq_ref, dk_ref, dv_ref):
    mask = causal(q_ref.shape[0])
    for h in range(q_ref.shape[1] // DH):
        g = g_ref[:, head(h)]
        back = jnp.where(mask, mm(g, v_ref[:, head(h)], 1, 1), 0.0).astype(BF16)
        near = mm(back, k_ref[:, head(h)], 1, 0)
        far = mm(g, prior_ref[:, head(h)], 1, 1)
        dq_ref[:, head(h)] = (scale * (near + far)).astype(BF16)
        dk_ref[:, head(h)] = mm(back, q_ref[:, head(h)], 0, 0)
        dv_ref[:, head(h)] = mm(attn_ref[h], g, 0, 0)


def outer_grads_kernel(scale, k_ref, v_ref, later_ref, near_k_ref, near_v_ref, dk_ref, dv_ref):
    for h in range(k_ref.shape[1] // DH):
        later = later_ref[head(h), :]
        far_k = mm(v_ref[:, head(h)], later, 1, 1)
        dk_ref[:, head(h)] = (scale * (near_k_ref[:, head(h)] + far_k)).astype(BF16)
        far_v = mm(k_ref[:, head(h)], later, 1, 0)
        dv_ref[:, head(h)] = (scale * (near_v_ref[:, head(h)] + far_v)).astype(BF16)


def shape(dims, dtype):
    return jax.ShapeDtypeStruct(dims, dtype)


def in_hbm(x):
    return pltpu.with_memory_space_constraint(x, pltpu.HBM)


def join(place, totals, part):
    return local_call(
        join_kernel,
        shape(part.shape, BF16),
        0,
        3 * part.size * 4,
        in_specs=[
            pl.BlockSpec(memory_space=pltpu.SMEM),
            pl.BlockSpec(memory_space=pltpu.VMEM),
            pl.BlockSpec(memory_space=pltpu.VMEM),
        ],
    )(place, totals, part)


def per_device(queries, keys, values, out_cotangent, proj_weight):
    tok, width = queries.shape
    heads = width // DH
    ny, nz = lax.axis_size("y"), lax.axis_size("z")
    nx, nc = lax.axis_size("x"), lax.axis_size("c")
    cols = out_cotangent.shape[1]
    scale = (DH * tok * ny * nz) ** -0.5
    place = lax.axis_index("y").reshape(1)
    weight_t = proj_weight.T
    own = weight_t.shape[0]
    share = DH // nz
    square = 2 * tok * DH * DH * heads
    wide = 2 * tok * tok * DH * heads
    big = tok * width

    sent = local_call(
        first_kernel, shape((nz, own + share, width), BF16), square, 3 * big
    )(in_hbm(keys), in_hbm(values), in_hbm(weight_t))
    got = exchange(sent, "z")
    weight_z, kv_part, kv_total = local_call(
        split_kernel,
        (
            shape((nz * own, width), BF16),
            shape((nz, share, width), F32),
            shape((ny, share, width), F32),
        ),
        0,
        2 * big,
    )(got)
    weight_full = lax.all_gather(weight_z, "y", axis=0, tiled=True)
    cot_own, kv_total = lax.optimization_barrier((out_cotangent, kv_total))
    cot_x = lax.all_gather(cot_own, "x")
    half = tok // 2
    cot_top = lax.all_gather(cot_x[:, :half], "c")
    cot_low = lax.all_gather(cot_x[:, half:], "c")
    attn, attn_inner = local_call(
        attn_kernel,
        (shape((heads, tok, tok), BF16), shape((tok, width), F32)),
        2 * wide,
        10 * big,
    )(queries, keys, values)
    prior = exchange(join(place, exchange(kv_total, "y"), kv_part), "z").reshape(DH, width)

    n_blocks = nx * nc
    whole = pl.BlockSpec((tok, width), lambda i: (0, 0))
    cot_spec = pl.BlockSpec((1, nx, half, cols), lambda i: (i, 0, 0, 0))
    by_core = pl.BlockSpec((nx, 1, cols, width), lambda i: (0, i, 0, 0))
    attn_out = local_call(
        functools.partial(attn_out_kernel, scale), shape((tok, width), BF16), square, 8 * big
    )(queries, prior, attn_inner)
    attn_out_y = lax.all_gather(attn_out, "y", axis=0, tiled=True)
    turn = [(y * n_blocks + t, t * ny + y) for y in range(ny) for t in range(n_blocks)]
    cot_turned = lax.ppermute(cot_own, ("y", "x", "c"), turn)

    grad_out, qg = local_call(
        grad_out_kernel,
        (shape((tok, width), BF16), shape((heads * DH, DH), BF16)),
        square + 2 * tok * cols * width * n_blocks,
        2 * n_blocks * cols * width,
        grid=(nc,),
        in_specs=[cot_spec, cot_spec, by_core, whole],
        out_specs=[whole, pl.BlockSpec((heads * DH, DH), lambda i: (0, 0))],
        scratch_shapes=[pltpu.VMEM((tok, width), F32)],
    )(cot_top, cot_low, in_hbm(weight_full.reshape(nx, nc, cols, width)), queries)
    qg, cot_turned = lax.optimization_barrier((qg, cot_turned))
    turned_x = lax.all_gather(cot_turned, "x")
    turned_top = lax.all_gather(turned_x[:, :half], "c")
    turned_low = lax.all_gather(turned_x[:, half:], "c")
    pieces = (ny * nz, heads * DH // (ny * nz), DH)
    qg_got = exchange(qg.reshape(pieces), SEQ)
    later_sums = local_call(later_kernel, shape(pieces, BF16), 0, 2 * big)(qg_got)
    grad_q, near_k, near_v = local_call(
        functools.partial(inner_grads_kernel, scale),
        (shape((tok, width), BF16), shape((tok, width), F32), shape((tok, width), F32)),
        4 * wide + square,
        16 * big,
    )(queries, keys, values, grad_out, attn, prior)
    later = exchange(later_sums, SEQ).reshape(heads * DH, DH)
    grad_k, grad_v = local_call(
        functools.partial(outer_grads_kernel, scale),
        (shape((tok, width), BF16), shape((tok, width), BF16)),
        2 * square,
        12 * big,
    )(keys, values, later, near_k, near_v)

    proj_part = local_call(
        proj_kernel,
        shape((cols, width), BF16),
        2 * tok * cols * width * n_blocks,
        24 * big,
        grid=(nc,),
        in_specs=[by_core, cot_spec, cot_spec],
        out_specs=pl.BlockSpec((cols, width), lambda i: (0, 0)),
        scratch_shapes=[pltpu.VMEM((cols, width), F32)],
    )(in_hbm(attn_out_y.reshape(nx, nc, tok, width)), turned_top, turned_low)
    proj_parts = exchange(proj_part.reshape(nz, own, width), "z")
    proj_sum = jnp.sum(proj_parts.astype(F32), axis=0)
    grad_proj = (proj_sum / jnp.sqrt(F32(tok * ny * nz))).T
    return grad_q, grad_k, grad_v, grad_proj


def solution(mesh):
    seq, tp = mesh.devices.shape
    inner, cores = 8, 2
    grid = Mesh(
        mesh.devices.reshape(seq // inner, inner, tp // cores, cores), ("y", "z", "x", "c")
    )
    tokens, weight = P(SEQ, ("x", "c")), P(("x", "c"), SEQ)
    return jax.shard_map(
        per_device,
        mesh=grid,
        in_specs=(tokens, tokens, tokens, tokens, weight),
        out_specs=(tokens, tokens, tokens, weight),
        check_vma=False,
    )
```

```python
import functools

import jax
import jax.numpy as jnp
from jax import lax
from jax.experimental import pallas as pl
from jax.experimental.pallas import tpu as pltpu
from jax.sharding import Mesh, PartitionSpec as P

DH = 128
SEQ = ("y", "z")
BF16 = jnp.bfloat16
F32 = jnp.float32
VMEM_BYTES = 24 * 1024 * 1024


def mm(a, b, ca, cb):
    return lax.dot_general(a, b, (((ca,), (cb,)), ((), ())), preferred_element_type=F32)


def head(h):
    return slice(h * DH, (h + 1) * DH)


def local_call(kernel, out_shape, flops, moved, **kwargs):
    return pl.pallas_call(
        kernel,
        out_shape=out_shape,
        cost_estimate=pl.CostEstimate(flops=flops, transcendentals=0, bytes_accessed=moved),
        compiler_params=pltpu.CompilerParams(vmem_limit_bytes=VMEM_BYTES),
        **kwargs,
    )


def causal(tok):
    rows = lax.broadcasted_iota(jnp.int32, (tok, tok), 0)
    cols = lax.broadcasted_iota(jnp.int32, (tok, tok), 1)
    return rows >= cols


def exchange(x, axis):
    return lax.all_to_all(x, axis, 0, 0, tiled=True)


def spread_kernel(w_ref, out_ref):
    for p in range(out_ref.shape[0]):
        out_ref[p] = w_ref[...]


def kv_kernel(k_ref, v_ref, out_ref):
    share = out_ref.shape[1] // 2
    per_head = DH // share
    for h in range(k_ref.shape[1] // DH):
        kv = mm(k_ref[:, head(h)], v_ref[:, head(h)], 0, 0)
        high = kv.astype(BF16)
        low = (kv - high.astype(F32)).astype(BF16)
        for i in range(per_head):
            piece = slice(i * share, (i + 1) * share)
            out_ref[h * per_head + i, :share, :] = high[piece]
            out_ref[h * per_head + i, share:, :] = low[piece]


def prior_kernel(got_ref, sums_ref):
    count, share, _ = sums_ref.shape
    at = got_ref.shape[1] - 2 * share
    running = jnp.zeros(sums_ref.shape[1:], F32)
    for s in range(count):
        sums_ref[s] = running.astype(BF16)
        high = got_ref[s, at : at + share, :].astype(F32)
        running = running + (high + got_ref[s, at + share :, :].astype(F32))


def later_kernel(got_ref, sums_ref):
    running = jnp.zeros(sums_ref.shape[1:], F32)
    for s in reversed(range(sums_ref.shape[0])):
        sums_ref[s] = running.astype(BF16)
        running = running + got_ref[s].astype(F32)


def attn_kernel(q_ref, k_ref, v_ref, attn_ref, inner_ref):
    mask = causal(q_ref.shape[0])
    for h in range(q_ref.shape[1] // DH):
        scores = mm(q_ref[:, head(h)], k_ref[:, head(h)], 1, 1)
        attn = jnp.where(mask, scores, 0.0).astype(BF16)
        attn_ref[h] = attn
        inner_ref[:, head(h)] = mm(attn, v_ref[:, head(h)], 1, 0)


def proj_kernel(scale, q_ref, prior_ref, inner_ref, top_ref, low_ref, out_ref, attn_out_ref):
    @pl.when(pl.program_id(0) == 0)
    def _():
        for h in range(q_ref.shape[1] // DH):
            far = mm(q_ref[:, head(h)], prior_ref[head(h), :], 1, 0)
            attn_out_ref[:, head(h)] = (scale * (inner_ref[:, head(h)] + far)).astype(BF16)

    for x in range(out_ref.shape[0]):
        cot = jnp.concatenate([top_ref[0, x], low_ref[0, x]], axis=0)
        out_ref[x, 0] = mm(cot, attn_out_ref[...], 0, 0).astype(BF16)


def grad_out_kernel(top_ref, low_ref, w_ref, q_ref, g_ref, qg_ref, acc_ref):
    step = pl.program_id(0)
    term = None
    for x in range(w_ref.shape[0]):
        cot = jnp.concatenate([top_ref[0, x], low_ref[0, x]], axis=0)
        one = mm(cot, w_ref[x, 0], 1, 0)
        term = one if term is None else term + one

    @pl.when(step == 0)
    def _():
        acc_ref[...] = term

    @pl.when(step > 0)
    def _():
        acc_ref[...] += term

    @pl.when(step == pl.num_programs(0) - 1)
    def _():
        g = acc_ref[...].astype(BF16)
        g_ref[...] = g
        for h in range(g.shape[1] // DH):
            qg_ref[head(h), :] = mm(q_ref[:, head(h)], g[:, head(h)], 0, 0).astype(BF16)


def inner_grads_kernel(scale, q_ref, k_ref, v_ref, g_ref, attn_ref, prior_ref, dq_ref, dk_ref, dv_ref):
    mask = causal(q_ref.shape[0])
    for h in range(q_ref.shape[1] // DH):
        g = g_ref[:, head(h)]
        back = jnp.where(mask, mm(g, v_ref[:, head(h)], 1, 1), 0.0).astype(BF16)
        near = mm(back, k_ref[:, head(h)], 1, 0)
        far = mm(g, prior_ref[head(h), :], 1, 1)
        dq_ref[:, head(h)] = (scale * (near + far)).astype(BF16)
        dk_ref[:, head(h)] = mm(back, q_ref[:, head(h)], 0, 0)
        dv_ref[:, head(h)] = mm(attn_ref[h], g, 0, 0)


def outer_grads_kernel(scale, k_ref, v_ref, later_ref, near_k_ref, near_v_ref, dk_ref, dv_ref):
    for h in range(k_ref.shape[1] // DH):
        later = later_ref[head(h), :]
        far_k = mm(v_ref[:, head(h)], later, 1, 1)
        dk_ref[:, head(h)] = (scale * (near_k_ref[:, head(h)] + far_k)).astype(BF16)
        far_v = mm(k_ref[:, head(h)], later, 1, 0)
        dv_ref[:, head(h)] = (scale * (near_v_ref[:, head(h)] + far_v)).astype(BF16)


def shape(dims, dtype):
    return jax.ShapeDtypeStruct(dims, dtype)


def in_hbm(x):
    return pltpu.with_memory_space_constraint(x, pltpu.HBM)


def per_device(queries, keys, values, out_cotangent, proj_weight):
    tok, width = queries.shape
    heads = width // DH
    ny, nz = lax.axis_size("y"), lax.axis_size("z")
    nx, nc = lax.axis_size("x"), lax.axis_size("c")
    cols = out_cotangent.shape[1]
    scale = (DH * tok * ny * nz) ** -0.5
    weight_t = proj_weight.T
    own = weight_t.shape[0]
    share = heads * DH // (ny * nz)
    square = 2 * tok * DH * DH * heads
    wide = 2 * tok * tok * DH * heads
    big = tok * width
    pieces = (ny * nz, share, DH)

    spread = local_call(spread_kernel, shape((nz, own, width), BF16), 0, big)(in_hbm(weight_t))
    weight_z = exchange(spread, "z").reshape(nz * own, width)
    weight_full = lax.all_gather(weight_z, "y", axis=0, tiled=True)
    kv_pieces = local_call(
        kv_kernel, shape((ny * nz, 2 * share, DH), BF16), square, 3 * big
    )(in_hbm(keys), in_hbm(values))
    kv_pieces, cot_own, weight_z = lax.optimization_barrier((kv_pieces, out_cotangent, weight_z))
    got = exchange(kv_pieces, SEQ)
    cot_x = lax.all_gather(cot_own, "x")
    got, cot_x = lax.optimization_barrier((got, cot_x))
    half = tok // 2
    cot_top = lax.all_gather(cot_x[:, :half], "c")
    cot_low = lax.all_gather(cot_x[:, half:], "c")
    attn, attn_inner = local_call(
        attn_kernel,
        (shape((heads, tok, tok), BF16), shape((tok, width), F32)),
        2 * wide,
        10 * big,
    )(queries, keys, values)
    sums = local_call(prior_kernel, shape(pieces, BF16), 0, 2 * big)(got)
    prior = exchange(sums, SEQ).reshape(heads * DH, DH)

    n_blocks = nx * nc

    whole = pl.BlockSpec((tok, width), lambda i: (0, 0))
    state = pl.BlockSpec((heads * DH, DH), lambda i: (0, 0))
    cot_spec = pl.BlockSpec((1, nx, half, cols), lambda i: (i, 0, 0, 0))
    by_core = pl.BlockSpec((nx, 1, cols, width), lambda i: (0, i, 0, 0))
    proj_term = local_call(
        functools.partial(proj_kernel, scale),
        pltpu.HBM((nx, nc, cols, width), BF16),
        square + 2 * tok * cols * width * n_blocks,
        2 * n_blocks * cols * width,
        grid=(nc,),
        in_specs=[whole, state, whole, cot_spec, cot_spec],
        out_specs=by_core,
        scratch_shapes=[pltpu.VMEM((tok, width), BF16)],
    )(queries, prior, attn_inner, cot_top, cot_low)
    proj_term = proj_term.reshape(n_blocks * cols, width)
    proj_y = lax.psum_scatter(proj_term, "y", scatter_dimension=0, tiled=True)

    grad_out, qg = local_call(
        grad_out_kernel,
        (shape((tok, width), BF16), shape((heads * DH, DH), BF16)),
        square + 2 * tok * cols * width * n_blocks,
        2 * n_blocks * cols * width,
        grid=(nc,),
        in_specs=[cot_spec, cot_spec, by_core, whole],
        out_specs=[whole, state],
        scratch_shapes=[pltpu.VMEM((tok, width), F32)],
    )(cot_top, cot_low, in_hbm(weight_full.reshape(nx, nc, cols, width)), queries)
    qg_got = exchange(qg.reshape(pieces), SEQ)
    sums = local_call(later_kernel, shape(pieces, BF16), 0, 2 * big)(qg_got)
    grad_q, near_k, near_v = local_call(
        functools.partial(inner_grads_kernel, scale),
        (shape((tok, width), BF16), shape((tok, width), F32), shape((tok, width), F32)),
        4 * wide + square,
        16 * big,
    )(queries, keys, values, grad_out, attn, prior)
    later = exchange(sums, SEQ).reshape(heads * DH, DH)
    grad_k, grad_v = local_call(
        functools.partial(outer_grads_kernel, scale),
        (shape((tok, width), BF16), shape((tok, width), BF16)),
        2 * square,
        12 * big,
    )(keys, values, later, near_k, near_v)

    proj_parts = exchange(proj_y.reshape(nz, own, width), "z")
    proj_sum = jnp.sum(proj_parts.astype(F32), axis=0)
    grad_proj = (proj_sum / jnp.sqrt(F32(tok * ny * nz))).T
    return grad_q, grad_k, grad_v, grad_proj


def solution(mesh):
    seq, tp = mesh.devices.shape
    inner, cores = 8, 2
    grid = Mesh(
        mesh.devices.reshape(seq // inner, inner, tp // cores, cores), ("y", "z", "x", "c")
    )
    tokens, weight = P(SEQ, ("x", "c")), P(("x", "c"), SEQ)
    return jax.shard_map(
        per_device,
        mesh=grid,
        in_specs=(tokens, tokens, tokens, tokens, weight),
        out_specs=(tokens, tokens, tokens, weight),
        check_vma=False,
    )
```

```python
import functools

import jax
import jax.numpy as jnp
from jax import lax
from jax.experimental import pallas as pl
from jax.experimental.pallas import tpu as pltpu
from jax.sharding import Mesh, PartitionSpec as P

DH = 128
SEQ = ("y", "z")
BF16 = jnp.bfloat16
F32 = jnp.float32
VMEM_BYTES = 24 * 1024 * 1024


def mm(a, b, ca, cb):
    return lax.dot_general(a, b, (((ca,), (cb,)), ((), ())), preferred_element_type=F32)


def head(h):
    return slice(h * DH, (h + 1) * DH)


def local_call(kernel, out_shape, flops, moved, **kwargs):
    return pl.pallas_call(
        kernel,
        out_shape=out_shape,
        cost_estimate=pl.CostEstimate(flops=flops, transcendentals=0, bytes_accessed=moved),
        compiler_params=pltpu.CompilerParams(vmem_limit_bytes=VMEM_BYTES),
        **kwargs,
    )


def causal(tok):
    rows = lax.broadcasted_iota(jnp.int32, (tok, tok), 0)
    cols = lax.broadcasted_iota(jnp.int32, (tok, tok), 1)
    return rows >= cols


def exchange(x, axis):
    return lax.all_to_all(x, axis, 0, 0, tiled=True)


def spread_kernel(w_ref, out_ref):
    for p in range(out_ref.shape[0]):
        out_ref[p] = w_ref[...]


def kv_kernel(k_ref, v_ref, out_ref):
    for h in range(k_ref.shape[1] // DH):
        out_ref[:, head(h)] = mm(k_ref[:, head(h)], v_ref[:, head(h)], 0, 0)


def part_kernel(got_ref, part_ref, total_ref):
    running = jnp.zeros(got_ref.shape[1:], F32)
    for p in range(got_ref.shape[0]):
        part_ref[p] = running
        running = running + got_ref[p]
    for p in range(total_ref.shape[0]):
        total_ref[p] = running


def join_kernel(place_ref, totals_ref, part_ref, out_ref):
    place = place_ref[0]
    base = jnp.zeros(totals_ref.shape[1:], F32)
    for other in range(totals_ref.shape[0]):
        counts = place > other
        base = base + jnp.where(counts, totals_ref[other], 0.0)
    for p in range(part_ref.shape[0]):
        out_ref[p] = (base + part_ref[p]).astype(out_ref.dtype)


def later_kernel(got_ref, sums_ref):
    running = jnp.zeros(sums_ref.shape[1:], F32)
    for s in reversed(range(sums_ref.shape[0])):
        sums_ref[s] = running.astype(BF16)
        running = running + got_ref[s].astype(F32)


def attn_kernel(q_ref, k_ref, v_ref, attn_ref, inner_ref):
    mask = causal(q_ref.shape[0])
    for h in range(q_ref.shape[1] // DH):
        scores = mm(q_ref[:, head(h)], k_ref[:, head(h)], 1, 1)
        attn = jnp.where(mask, scores, 0.0).astype(BF16)
        attn_ref[h] = attn
        inner_ref[:, head(h)] = mm(attn, v_ref[:, head(h)], 1, 0)


def proj_kernel(scale, q_ref, prior_ref, inner_ref, top_ref, low_ref, out_ref, attn_out_ref):
    @pl.when(pl.program_id(0) == 0)
    def _():
        for h in range(q_ref.shape[1] // DH):
            far = mm(q_ref[:, head(h)], prior_ref[:, head(h)], 1, 0)
            attn_out_ref[:, head(h)] = (scale * (inner_ref[:, head(h)] + far)).astype(BF16)

    for x in range(out_ref.shape[0]):
        cot = jnp.concatenate([top_ref[0, x], low_ref[0, x]], axis=0)
        out_ref[x, 0] = mm(cot, attn_out_ref[...], 0, 0).astype(BF16)


def grad_out_kernel(top_ref, low_ref, w_ref, q_ref, g_ref, qg_ref, acc_ref):
    step = pl.program_id(0)
    term = None
    for x in range(w_ref.shape[0]):
        cot = jnp.concatenate([top_ref[0, x], low_ref[0, x]], axis=0)
        one = mm(cot, w_ref[x, 0], 1, 0)
        term = one if term is None else term + one

    @pl.when(step == 0)
    def _():
        acc_ref[...] = term

    @pl.when(step > 0)
    def _():
        acc_ref[...] += term

    @pl.when(step == pl.num_programs(0) - 1)
    def _():
        g = acc_ref[...].astype(BF16)
        g_ref[...] = g
        for h in range(g.shape[1] // DH):
            qg_ref[head(h), :] = mm(q_ref[:, head(h)], g[:, head(h)], 0, 0).astype(BF16)


def inner_grads_kernel(scale, q_ref, k_ref, v_ref, g_ref, attn_ref, prior_ref, dq_ref, dk_ref, dv_ref):
    mask = causal(q_ref.shape[0])
    for h in range(q_ref.shape[1] // DH):
        g = g_ref[:, head(h)]
        back = jnp.where(mask, mm(g, v_ref[:, head(h)], 1, 1), 0.0).astype(BF16)
        near = mm(back, k_ref[:, head(h)], 1, 0)
        far = mm(g, prior_ref[:, head(h)], 1, 1)
        dq_ref[:, head(h)] = (scale * (near + far)).astype(BF16)
        dk_ref[:, head(h)] = mm(back, q_ref[:, head(h)], 0, 0)
        dv_ref[:, head(h)] = mm(attn_ref[h], g, 0, 0)


def outer_grads_kernel(scale, k_ref, v_ref, later_ref, near_k_ref, near_v_ref, dk_ref, dv_ref):
    for h in range(k_ref.shape[1] // DH):
        later = later_ref[head(h), :]
        far_k = mm(v_ref[:, head(h)], later, 1, 1)
        dk_ref[:, head(h)] = (scale * (near_k_ref[:, head(h)] + far_k)).astype(BF16)
        far_v = mm(k_ref[:, head(h)], later, 1, 0)
        dv_ref[:, head(h)] = (scale * (near_v_ref[:, head(h)] + far_v)).astype(BF16)


def shape(dims, dtype):
    return jax.ShapeDtypeStruct(dims, dtype)


def in_hbm(x):
    return pltpu.with_memory_space_constraint(x, pltpu.HBM)


def join(place, totals, part):
    return local_call(
        join_kernel,
        shape(part.shape, BF16),
        0,
        3 * part.size * 4,
        in_specs=[
            pl.BlockSpec(memory_space=pltpu.SMEM),
            pl.BlockSpec(memory_space=pltpu.VMEM),
            pl.BlockSpec(memory_space=pltpu.VMEM),
        ],
    )(place, totals, part)


def per_device(queries, keys, values, out_cotangent, proj_weight):
    tok, width = queries.shape
    heads = width // DH
    ny, nz = lax.axis_size("y"), lax.axis_size("z")
    nx, nc = lax.axis_size("x"), lax.axis_size("c")
    cols = out_cotangent.shape[1]
    scale = (DH * tok * ny * nz) ** -0.5
    place = lax.axis_index("y").reshape(1)
    weight_t = proj_weight.T
    own = weight_t.shape[0]
    share = heads * DH // (ny * nz)
    square = 2 * tok * DH * DH * heads
    wide = 2 * tok * tok * DH * heads
    big = tok * width
    pieces = (ny * nz, share, DH)

    spread = local_call(spread_kernel, shape((nz, own, width), BF16), 0, big)(in_hbm(weight_t))
    weight_z = exchange(spread, "z").reshape(nz * own, width)
    kv = local_call(kv_kernel, shape((DH, width), F32), square, 3 * big)(
        in_hbm(keys), in_hbm(values)
    )
    kv, cot_own, weight_z = lax.optimization_barrier((kv, out_cotangent, weight_z))
    weight_full = lax.all_gather(weight_z, "y", axis=0, tiled=True)
    got = exchange(kv.reshape(nz, DH // nz, width), "z")
    cot_x = lax.all_gather(cot_own, "x")
    got, cot_x = lax.optimization_barrier((got, cot_x))
    kv_part, kv_total = local_call(
        part_kernel,
        (shape(got.shape, F32), shape((ny,) + got.shape[1:], F32)),
        0,
        2 * big,
    )(got)
    half = tok // 2
    cot_top = lax.all_gather(cot_x[:, :half], "c")
    cot_low = lax.all_gather(cot_x[:, half:], "c")
    attn, attn_inner = local_call(
        attn_kernel,
        (shape((heads, tok, tok), BF16), shape((tok, width), F32)),
        2 * wide,
        10 * big,
    )(queries, keys, values)
    prior = exchange(join(place, exchange(kv_total, "y"), kv_part), "z").reshape(DH, width)

    n_blocks = nx * nc

    whole = pl.BlockSpec((tok, width), lambda i: (0, 0))
    state = pl.BlockSpec((DH, width), lambda i: (0, 0))
    cot_spec = pl.BlockSpec((1, nx, half, cols), lambda i: (i, 0, 0, 0))
    by_core = pl.BlockSpec((nx, 1, cols, width), lambda i: (0, i, 0, 0))
    proj_term = local_call(
        functools.partial(proj_kernel, scale),
        pltpu.HBM((nx, nc, cols, width), BF16),
        square + 2 * tok * cols * width * n_blocks,
        2 * n_blocks * cols * width,
        grid=(nc,),
        in_specs=[whole, state, whole, cot_spec, cot_spec],
        out_specs=by_core,
        scratch_shapes=[pltpu.VMEM((tok, width), BF16)],
    )(queries, prior, attn_inner, cot_top, cot_low)
    proj_term = proj_term.reshape(n_blocks * cols, width)
    proj_y = lax.psum_scatter(proj_term, "y", scatter_dimension=0, tiled=True)

    grad_out, qg = local_call(
        grad_out_kernel,
        (shape((tok, width), BF16), shape((heads * DH, DH), BF16)),
        square + 2 * tok * cols * width * n_blocks,
        2 * n_blocks * cols * width,
        grid=(nc,),
        in_specs=[cot_spec, cot_spec, by_core, whole],
        out_specs=[whole, pl.BlockSpec((heads * DH, DH), lambda i: (0, 0))],
        scratch_shapes=[pltpu.VMEM((tok, width), F32)],
    )(cot_top, cot_low, in_hbm(weight_full.reshape(nx, nc, cols, width)), queries)
    qg_got = exchange(qg.reshape(pieces), SEQ)
    sums = local_call(later_kernel, shape(pieces, BF16), 0, 2 * big)(qg_got)
    grad_q, near_k, near_v = local_call(
        functools.partial(inner_grads_kernel, scale),
        (shape((tok, width), BF16), shape((tok, width), F32), shape((tok, width), F32)),
        4 * wide + square,
        16 * big,
    )(queries, keys, values, grad_out, attn, prior)
    later = exchange(sums, SEQ).reshape(heads * DH, DH)
    grad_k, grad_v = local_call(
        functools.partial(outer_grads_kernel, scale),
        (shape((tok, width), BF16), shape((tok, width), BF16)),
        2 * square,
        12 * big,
    )(keys, values, later, near_k, near_v)

    proj_parts = exchange(proj_y.reshape(nz, own, width), "z")
    proj_sum = jnp.sum(proj_parts.astype(F32), axis=0)
    grad_proj = (proj_sum / jnp.sqrt(F32(tok * ny * nz))).T
    return grad_q, grad_k, grad_v, grad_proj


def solution(mesh):
    seq, tp = mesh.devices.shape
    inner, cores = 8, 2
    grid = Mesh(
        mesh.devices.reshape(seq // inner, inner, tp // cores, cores), ("y", "z", "x", "c")
    )
    tokens, weight = P(SEQ, ("x", "c")), P(("x", "c"), SEQ)
    return jax.shard_map(
        per_device,
        mesh=grid,
        in_specs=(tokens, tokens, tokens, tokens, weight),
        out_specs=(tokens, tokens, tokens, weight),
        check_vma=False,
    )
```

```python
import functools

import jax
import jax.numpy as jnp
from jax import lax
from jax.experimental import pallas as pl
from jax.experimental.pallas import tpu as pltpu
from jax.sharding import Mesh, PartitionSpec as P

DH = 128
SEQ = ("y", "z")
BF16 = jnp.bfloat16
F32 = jnp.float32
VMEM_BYTES = 24 * 1024 * 1024


def mm(a, b, ca, cb):
    return lax.dot_general(a, b, (((ca,), (cb,)), ((), ())), preferred_element_type=F32)


def head(h):
    return slice(h * DH, (h + 1) * DH)


def local_call(kernel, out_shape, flops, moved, **kwargs):
    return pl.pallas_call(
        kernel,
        out_shape=out_shape,
        cost_estimate=pl.CostEstimate(flops=flops, transcendentals=0, bytes_accessed=moved),
        compiler_params=pltpu.CompilerParams(vmem_limit_bytes=VMEM_BYTES),
        **kwargs,
    )


def causal(tok):
    rows = lax.broadcasted_iota(jnp.int32, (tok, tok), 0)
    cols = lax.broadcasted_iota(jnp.int32, (tok, tok), 1)
    return rows >= cols


def exchange(x, axis):
    return lax.all_to_all(x, axis, 0, 0, tiled=True)


def first_kernel(k_ref, v_ref, w_ref, out_ref):
    peers, rows, width = out_ref.shape
    own = w_ref.shape[0]
    share = (rows - own) // 2
    for h in range(width // DH):
        kv = mm(k_ref[:, head(h)], v_ref[:, head(h)], 0, 0)
        high = kv.astype(BF16)
        low = (kv - high.astype(F32)).astype(BF16)
        for p in range(peers):
            out_ref[p, own : own + share, head(h)] = high[p * share : (p + 1) * share]
            out_ref[p, own + share :, head(h)] = low[p * share : (p + 1) * share]
    for p in range(peers):
        out_ref[p, :own, :] = w_ref[...]


def split_kernel(got_ref, weight_ref, part_ref, total_ref):
    peers, rows, width = got_ref.shape
    own = weight_ref.shape[0] // peers
    share = (rows - own) // 2
    running = jnp.zeros((share, width), F32)
    for p in range(peers):
        weight_ref[p * own : (p + 1) * own, :] = got_ref[p, :own, :]
        part_ref[p] = running
        high = got_ref[p, own : own + share, :].astype(F32)
        running = running + (high + got_ref[p, own + share :, :].astype(F32))
    for p in range(total_ref.shape[0]):
        total_ref[p] = running


def later_kernel(got_ref, sums_ref):
    running = jnp.zeros(sums_ref.shape[1:], F32)
    for s in reversed(range(sums_ref.shape[0])):
        sums_ref[s] = running.astype(BF16)
        running = running + got_ref[s].astype(F32)


def join_kernel(place_ref, totals_ref, part_ref, out_ref):
    place = place_ref[0]
    base = jnp.zeros(totals_ref.shape[1:], F32)
    for other in range(totals_ref.shape[0]):
        counts = place > other
        base = base + jnp.where(counts, totals_ref[other], 0.0)
    for p in range(part_ref.shape[0]):
        out_ref[p] = (base + part_ref[p]).astype(out_ref.dtype)


def attn_kernel(q_ref, k_ref, v_ref, attn_ref, inner_ref):
    mask = causal(q_ref.shape[0])
    for h in range(q_ref.shape[1] // DH):
        scores = mm(q_ref[:, head(h)], k_ref[:, head(h)], 1, 1)
        attn = jnp.where(mask, scores, 0.0).astype(BF16)
        attn_ref[h] = attn
        inner_ref[:, head(h)] = mm(attn, v_ref[:, head(h)], 1, 0)


def proj_kernel(scale, q_ref, prior_ref, inner_ref, top_ref, low_ref, out_ref, attn_out_ref):
    @pl.when(pl.program_id(0) == 0)
    def _():
        for h in range(q_ref.shape[1] // DH):
            far = mm(q_ref[:, head(h)], prior_ref[:, head(h)], 1, 0)
            attn_out_ref[:, head(h)] = (scale * (inner_ref[:, head(h)] + far)).astype(BF16)

    for x in range(out_ref.shape[0]):
        cot = jnp.concatenate([top_ref[0, x], low_ref[0, x]], axis=0)
        out_ref[x, 0] = mm(cot, attn_out_ref[...], 0, 0).astype(BF16)


def grad_out_kernel(top_ref, low_ref, w_ref, q_ref, g_ref, qg_ref, acc_ref):
    step = pl.program_id(0)
    term = None
    for x in range(w_ref.shape[0]):
        cot = jnp.concatenate([top_ref[0, x], low_ref[0, x]], axis=0)
        one = mm(cot, w_ref[x, 0], 1, 0)
        term = one if term is None else term + one

    @pl.when(step == 0)
    def _():
        acc_ref[...] = term

    @pl.when(step > 0)
    def _():
        acc_ref[...] += term

    @pl.when(step == pl.num_programs(0) - 1)
    def _():
        g = acc_ref[...].astype(BF16)
        g_ref[...] = g
        for h in range(g.shape[1] // DH):
            qg_ref[head(h), :] = mm(q_ref[:, head(h)], g[:, head(h)], 0, 0).astype(BF16)


def inner_grads_kernel(scale, q_ref, k_ref, v_ref, g_ref, attn_ref, prior_ref, dq_ref, dk_ref, dv_ref):
    mask = causal(q_ref.shape[0])
    for h in range(q_ref.shape[1] // DH):
        g = g_ref[:, head(h)]
        back = jnp.where(mask, mm(g, v_ref[:, head(h)], 1, 1), 0.0).astype(BF16)
        near = mm(back, k_ref[:, head(h)], 1, 0)
        far = mm(g, prior_ref[:, head(h)], 1, 1)
        dq_ref[:, head(h)] = (scale * (near + far)).astype(BF16)
        dk_ref[:, head(h)] = mm(back, q_ref[:, head(h)], 0, 0)
        dv_ref[:, head(h)] = mm(attn_ref[h], g, 0, 0)


def outer_grads_kernel(scale, k_ref, v_ref, later_ref, near_k_ref, near_v_ref, dk_ref, dv_ref):
    for h in range(k_ref.shape[1] // DH):
        later = later_ref[head(h), :]
        far_k = mm(v_ref[:, head(h)], later, 1, 1)
        dk_ref[:, head(h)] = (scale * (near_k_ref[:, head(h)] + far_k)).astype(BF16)
        far_v = mm(k_ref[:, head(h)], later, 1, 0)
        dv_ref[:, head(h)] = (scale * (near_v_ref[:, head(h)] + far_v)).astype(BF16)


def shape(dims, dtype):
    return jax.ShapeDtypeStruct(dims, dtype)


def in_hbm(x):
    return pltpu.with_memory_space_constraint(x, pltpu.HBM)


def join(place, totals, part):
    return local_call(
        join_kernel,
        shape(part.shape, BF16),
        0,
        3 * part.size * 4,
        in_specs=[
            pl.BlockSpec(memory_space=pltpu.SMEM),
            pl.BlockSpec(memory_space=pltpu.VMEM),
            pl.BlockSpec(memory_space=pltpu.VMEM),
        ],
    )(place, totals, part)


def per_device(queries, keys, values, out_cotangent, proj_weight):
    tok, width = queries.shape
    heads = width // DH
    ny, nz = lax.axis_size("y"), lax.axis_size("z")
    nx, nc = lax.axis_size("x"), lax.axis_size("c")
    cols = out_cotangent.shape[1]
    scale = (DH * tok * ny * nz) ** -0.5
    place = lax.axis_index("y").reshape(1)
    weight_t = proj_weight.T
    own = weight_t.shape[0]
    share = DH // nz
    square = 2 * tok * DH * DH * heads
    wide = 2 * tok * tok * DH * heads
    big = tok * width

    sent = local_call(
        first_kernel, shape((nz, own + 2 * share, width), BF16), square, 3 * big
    )(in_hbm(keys), in_hbm(values), in_hbm(weight_t))
    got = exchange(sent, "z")
    weight_z, kv_part, kv_total = local_call(
        split_kernel,
        (
            shape((nz * own, width), BF16),
            shape((nz, share, width), F32),
            shape((ny, share, width), F32),
        ),
        0,
        2 * big,
    )(got)
    weight_full = lax.all_gather(weight_z, "y", axis=0, tiled=True)
    cot_own, kv_total = lax.optimization_barrier((out_cotangent, kv_total))
    cot_x = lax.all_gather(cot_own, "x")
    half = tok // 2
    cot_top = lax.all_gather(cot_x[:, :half], "c")
    cot_low = lax.all_gather(cot_x[:, half:], "c")
    attn, attn_inner = local_call(
        attn_kernel,
        (shape((heads, tok, tok), BF16), shape((tok, width), F32)),
        2 * wide,
        10 * big,
    )(queries, keys, values)
    prior = exchange(join(place, exchange(kv_total, "y"), kv_part), "z")
    prior = prior.reshape(DH, width)

    n_blocks = nx * nc

    whole = pl.BlockSpec((tok, width), lambda i: (0, 0))
    state = pl.BlockSpec((DH, width), lambda i: (0, 0))
    cot_spec = pl.BlockSpec((1, nx, half, cols), lambda i: (i, 0, 0, 0))
    by_core = pl.BlockSpec((nx, 1, cols, width), lambda i: (0, i, 0, 0))
    proj_term = local_call(
        functools.partial(proj_kernel, scale),
        pltpu.HBM((nx, nc, cols, width), BF16),
        square + 2 * tok * cols * width * n_blocks,
        2 * n_blocks * cols * width,
        grid=(nc,),
        in_specs=[whole, state, whole, cot_spec, cot_spec],
        out_specs=by_core,
        scratch_shapes=[pltpu.VMEM((tok, width), BF16)],
    )(queries, prior, attn_inner, cot_top, cot_low)
    proj_term = proj_term.reshape(n_blocks * cols, width)
    proj_y = lax.psum_scatter(proj_term, "y", scatter_dimension=0, tiled=True)

    grad_out, qg = local_call(
        grad_out_kernel,
        (shape((tok, width), BF16), shape((heads * DH, DH), BF16)),
        square + 2 * tok * cols * width * n_blocks,
        2 * n_blocks * cols * width,
        grid=(nc,),
        in_specs=[cot_spec, cot_spec, by_core, whole],
        out_specs=[whole, pl.BlockSpec((heads * DH, DH), lambda i: (0, 0))],
        scratch_shapes=[pltpu.VMEM((tok, width), F32)],
    )(cot_top, cot_low, in_hbm(weight_full.reshape(nx, nc, cols, width)), queries)
    pieces = (ny * nz, heads * DH // (ny * nz), DH)
    qg_got = exchange(qg.reshape(pieces), SEQ)
    sums = local_call(later_kernel, shape(pieces, BF16), 0, 2 * big)(qg_got)
    grad_q, near_k, near_v = local_call(
        functools.partial(inner_grads_kernel, scale),
        (shape((tok, width), BF16), shape((tok, width), F32), shape((tok, width), F32)),
        4 * wide + square,
        16 * big,
    )(queries, keys, values, grad_out, attn, prior)
    later = exchange(sums, SEQ).reshape(heads * DH, DH)
    grad_k, grad_v = local_call(
        functools.partial(outer_grads_kernel, scale),
        (shape((tok, width), BF16), shape((tok, width), BF16)),
        2 * square,
        12 * big,
    )(keys, values, later, near_k, near_v)

    proj_parts = exchange(proj_y.reshape(nz, own, width), "z")
    proj_sum = jnp.sum(proj_parts.astype(F32), axis=0)
    grad_proj = (proj_sum / jnp.sqrt(F32(tok * ny * nz))).T
    return grad_q, grad_k, grad_v, grad_proj


def solution(mesh):
    seq, tp = mesh.devices.shape
    inner, cores = 8, 2
    grid = Mesh(
        mesh.devices.reshape(seq // inner, inner, tp // cores, cores), ("y", "z", "x", "c")
    )
    tokens, weight = P(SEQ, ("x", "c")), P(("x", "c"), SEQ)
    return jax.shard_map(
        per_device,
        mesh=grid,
        in_specs=(tokens, tokens, tokens, tokens, weight),
        out_specs=(tokens, tokens, tokens, weight),
        check_vma=False,
    )
```

```python
import functools

import jax
import jax.numpy as jnp
from jax import lax
from jax.experimental import pallas as pl
from jax.experimental.pallas import tpu as pltpu
from jax.sharding import Mesh, PartitionSpec as P

DH = 128
SEQ = ("y", "z")
BF16 = jnp.bfloat16
F32 = jnp.float32
VMEM_BYTES = 24 * 1024 * 1024


def mm(a, b, ca, cb):
    return lax.dot_general(a, b, (((ca,), (cb,)), ((), ())), preferred_element_type=F32)


def head(h):
    return slice(h * DH, (h + 1) * DH)


def local_call(kernel, out_shape, flops, moved, **kwargs):
    return pl.pallas_call(
        kernel,
        out_shape=out_shape,
        cost_estimate=pl.CostEstimate(flops=flops, transcendentals=0, bytes_accessed=moved),
        compiler_params=pltpu.CompilerParams(vmem_limit_bytes=VMEM_BYTES),
        **kwargs,
    )


def causal(tok):
    rows = lax.broadcasted_iota(jnp.int32, (tok, tok), 0)
    cols = lax.broadcasted_iota(jnp.int32, (tok, tok), 1)
    return rows >= cols


def exchange(x, axis):
    return lax.all_to_all(x, axis, 0, 0, tiled=True)


def spread_kernel(w_ref, out_ref):
    for p in range(out_ref.shape[0]):
        out_ref[p] = w_ref[...]


def kv_kernel(k_ref, v_ref, out_ref):
    for h in range(k_ref.shape[1] // DH):
        out_ref[:, head(h)] = mm(k_ref[:, head(h)], v_ref[:, head(h)], 0, 0)


def part_kernel(got_ref, part_ref, total_ref):
    running = jnp.zeros(got_ref.shape[1:], F32)
    for p in range(got_ref.shape[0]):
        part_ref[p] = running
        running = running + got_ref[p]
    for p in range(total_ref.shape[0]):
        total_ref[p] = running


def join_kernel(place_ref, totals_ref, part_ref, out_ref):
    place = place_ref[0]
    base = jnp.zeros(totals_ref.shape[1:], F32)
    for other in range(totals_ref.shape[0]):
        counts = place > other
        base = base + jnp.where(counts, totals_ref[other], 0.0)
    for p in range(part_ref.shape[0]):
        out_ref[p] = (base + part_ref[p]).astype(out_ref.dtype)


def later_kernel(got_ref, sums_ref):
    running = jnp.zeros(sums_ref.shape[1:], F32)
    for s in reversed(range(sums_ref.shape[0])):
        sums_ref[s] = running.astype(BF16)
        running = running + got_ref[s].astype(F32)


def attn_kernel(q_ref, k_ref, v_ref, attn_ref, inner_ref):
    mask = causal(q_ref.shape[0])
    for h in range(q_ref.shape[1] // DH):
        scores = mm(q_ref[:, head(h)], k_ref[:, head(h)], 1, 1)
        attn = jnp.where(mask, scores, 0.0).astype(BF16)
        attn_ref[h] = attn
        inner_ref[:, head(h)] = mm(attn, v_ref[:, head(h)], 1, 0)


def proj_kernel(scale, q_ref, prior_ref, inner_ref, top_ref, low_ref, out_ref, attn_out_ref):
    @pl.when((pl.program_id(0) == 0) & (pl.program_id(1) == 0))
    def _():
        for h in range(q_ref.shape[1] // DH):
            far = mm(q_ref[:, head(h)], prior_ref[:, head(h)], 1, 0)
            attn_out_ref[:, head(h)] = (scale * (inner_ref[:, head(h)] + far)).astype(BF16)

    for x in range(out_ref.shape[0]):
        cot = jnp.concatenate([top_ref[0, x], low_ref[0, x]], axis=0)
        out_ref[x, 0] = mm(cot, attn_out_ref[...], 0, 0).astype(BF16)


def grad_out_kernel(top_ref, low_ref, w_ref, q_ref, g_ref, qg_ref, acc_ref):
    step = pl.program_id(0)
    term = None
    for x in range(w_ref.shape[1]):
        cot = jnp.concatenate([top_ref[0, x], low_ref[0, x]], axis=0)
        one = mm(cot, w_ref[:, x, 0].reshape(cot.shape[1], w_ref.shape[4]), 1, 0)
        term = one if term is None else term + one

    @pl.when(step == 0)
    def _():
        acc_ref[...] = term

    @pl.when(step > 0)
    def _():
        acc_ref[...] += term

    @pl.when(step == pl.num_programs(0) - 1)
    def _():
        g = acc_ref[...].astype(BF16)
        g_ref[...] = g
        for h in range(g.shape[1] // DH):
            qg_ref[head(h), :] = mm(q_ref[:, head(h)], g[:, head(h)], 0, 0).astype(BF16)


def inner_grads_kernel(scale, q_ref, k_ref, v_ref, g_ref, attn_ref, prior_ref, dq_ref, dk_ref, dv_ref):
    mask = causal(q_ref.shape[0])
    for h in range(q_ref.shape[1] // DH):
        g = g_ref[:, head(h)]
        back = jnp.where(mask, mm(g, v_ref[:, head(h)], 1, 1), 0.0).astype(BF16)
        near = mm(back, k_ref[:, head(h)], 1, 0)
        far = mm(g, prior_ref[:, head(h)], 1, 1)
        dq_ref[:, head(h)] = (scale * (near + far)).astype(BF16)
        dk_ref[:, head(h)] = mm(back, q_ref[:, head(h)], 0, 0)
        dv_ref[:, head(h)] = mm(attn_ref[h], g, 0, 0)


def outer_grads_kernel(scale, k_ref, v_ref, later_ref, near_k_ref, near_v_ref, dk_ref, dv_ref):
    for h in range(k_ref.shape[1] // DH):
        later = later_ref[head(h), :]
        far_k = mm(v_ref[:, head(h)], later, 1, 1)
        dk_ref[:, head(h)] = (scale * (near_k_ref[:, head(h)] + far_k)).astype(BF16)
        far_v = mm(k_ref[:, head(h)], later, 1, 0)
        dv_ref[:, head(h)] = (scale * (near_v_ref[:, head(h)] + far_v)).astype(BF16)


def shape(dims, dtype):
    return jax.ShapeDtypeStruct(dims, dtype)


def in_hbm(x):
    return pltpu.with_memory_space_constraint(x, pltpu.HBM)


def join(place, totals, part):
    return local_call(
        join_kernel,
        shape(part.shape, BF16),
        0,
        3 * part.size * 4,
        in_specs=[
            pl.BlockSpec(memory_space=pltpu.SMEM),
            pl.BlockSpec(memory_space=pltpu.VMEM),
            pl.BlockSpec(memory_space=pltpu.VMEM),
        ],
    )(place, totals, part)


def per_device(queries, keys, values, out_cotangent, proj_weight):
    tok, width = queries.shape
    heads = width // DH
    ny, nz = lax.axis_size("y"), lax.axis_size("z")
    nx, nc = lax.axis_size("x"), lax.axis_size("c")
    cols = out_cotangent.shape[1]
    scale = (DH * tok * ny * nz) ** -0.5
    place = lax.axis_index("y").reshape(1)
    weight_t = proj_weight.T
    own = weight_t.shape[0]
    share = heads * DH // (ny * nz)
    square = 2 * tok * DH * DH * heads
    wide = 2 * tok * tok * DH * heads
    big = tok * width
    pieces = (ny * nz, share, DH)

    spread = local_call(spread_kernel, shape((ny, own, width), BF16), 0, big)(in_hbm(weight_t))
    weight_y = exchange(spread, "y").reshape(ny * own, width)
    kv = local_call(kv_kernel, shape((DH, width), F32), square, 3 * big)(
        in_hbm(keys), in_hbm(values)
    )
    kv, cot_own, weight_y = lax.optimization_barrier((kv, out_cotangent, weight_y))
    weight_full = lax.all_gather(weight_y, "z", axis=0, tiled=True)
    got = exchange(kv.reshape(nz, DH // nz, width), "z")
    cot_x = lax.all_gather(cot_own, "x")
    got, cot_x = lax.optimization_barrier((got, cot_x))
    kv_part, kv_total = local_call(
        part_kernel,
        (shape(got.shape, F32), shape((ny,) + got.shape[1:], F32)),
        0,
        2 * big,
    )(got)
    half = tok // 2
    cot_top = lax.all_gather(cot_x[:, :half], "c")
    cot_low = lax.all_gather(cot_x[:, half:], "c")
    attn, attn_inner = local_call(
        attn_kernel,
        (shape((heads, tok, tok), BF16), shape((tok, width), F32)),
        2 * wide,
        10 * big,
    )(queries, keys, values)
    prior = exchange(join(place, exchange(kv_total, "y"), kv_part), "z").reshape(DH, width)

    n_blocks = nx * nc

    whole = pl.BlockSpec((tok, width), lambda i: (0, 0))
    state = pl.BlockSpec((DH, width), lambda i: (0, 0))
    cot_spec = pl.BlockSpec((1, nx, half, cols), lambda i: (i, 0, 0, 0))
    by_core = pl.BlockSpec((nx, 1, cols, width), lambda i: (0, i, 0, 0))
    few = nx // 2
    cot_few = pl.BlockSpec((1, few, half, cols), lambda i, j: (i, j, 0, 0))
    same = pl.BlockSpec((tok, width), lambda i, j: (0, 0))
    proj_term = local_call(
        functools.partial(proj_kernel, scale),
        pltpu.HBM((nx, nc, cols, width), BF16),
        square + 2 * tok * cols * width * n_blocks,
        2 * n_blocks * cols * width,
        grid=(nc, nx // few),
        in_specs=[
            same,
            pl.BlockSpec((DH, width), lambda i, j: (0, 0)),
            same,
            cot_few,
            cot_few,
        ],
        out_specs=pl.BlockSpec((few, 1, cols, width), lambda i, j: (j, i, 0, 0)),
        scratch_shapes=[pltpu.VMEM((tok, width), BF16)],
    )(queries, prior, attn_inner, cot_top, cot_low)
    proj_term = proj_term.reshape(n_blocks * cols, width)
    proj_y = lax.psum_scatter(proj_term, "y", scatter_dimension=0, tiled=True)

    grad_out, qg = local_call(
        grad_out_kernel,
        (shape((tok, width), BF16), shape((heads * DH, DH), BF16)),
        square + 2 * tok * cols * width * n_blocks,
        2 * n_blocks * cols * width,
        grid=(nc,),
        in_specs=[
            cot_spec,
            cot_spec,
            pl.BlockSpec((nz, nx, 1, own, width), lambda i: (0, 0, i, 0, 0)),
            whole,
        ],
        out_specs=[whole, pl.BlockSpec((heads * DH, DH), lambda i: (0, 0))],
        scratch_shapes=[pltpu.VMEM((tok, width), F32)],
    )(cot_top, cot_low, in_hbm(weight_full.reshape(nz, nx, nc, own, width)), queries)
    qg_got = exchange(qg.reshape(pieces), SEQ)
    sums = local_call(later_kernel, shape(pieces, BF16), 0, 2 * big)(qg_got)
    grad_q, near_k, near_v = local_call(
        functools.partial(inner_grads_kernel, scale),
        (shape((tok, width), BF16), shape((tok, width), F32), shape((tok, width), F32)),
        4 * wide + square,
        16 * big,
    )(queries, keys, values, grad_out, attn, prior)
    later = exchange(sums, SEQ).reshape(heads * DH, DH)
    grad_k, grad_v = local_call(
        functools.partial(outer_grads_kernel, scale),
        (shape((tok, width), BF16), shape((tok, width), BF16)),
        2 * square,
        12 * big,
    )(keys, values, later, near_k, near_v)

    proj_parts = exchange(proj_y.reshape(nz, own, width), "z")
    proj_sum = jnp.sum(proj_parts.astype(F32), axis=0)
    grad_proj = (proj_sum / jnp.sqrt(F32(tok * ny * nz))).T
    return grad_q, grad_k, grad_v, grad_proj


def solution(mesh):
    seq, tp = mesh.devices.shape
    inner, cores = 8, 2
    grid = Mesh(
        mesh.devices.reshape(seq // inner, inner, tp // cores, cores), ("y", "z", "x", "c")
    )
    tokens, weight = P(SEQ, ("x", "c")), P(("x", "c"), SEQ)
    return jax.shard_map(
        per_device,
        mesh=grid,
        in_specs=(tokens, tokens, tokens, tokens, weight),
        out_specs=(tokens, tokens, tokens, weight),
        check_vma=False,
    )
```

```python
import functools

import jax
import jax.numpy as jnp
from jax import lax
from jax.experimental import pallas as pl
from jax.experimental.pallas import tpu as pltpu
from jax.sharding import Mesh, PartitionSpec as P

DH = 128
SEQ = ("y", "z")
BF16 = jnp.bfloat16
F32 = jnp.float32
VMEM_BYTES = 24 * 1024 * 1024


def mm(a, b, ca, cb):
    return lax.dot_general(a, b, (((ca,), (cb,)), ((), ())), preferred_element_type=F32)


def head(h):
    return slice(h * DH, (h + 1) * DH)


def local_call(kernel, out_shape, flops, moved, **kwargs):
    return pl.pallas_call(
        kernel,
        out_shape=out_shape,
        cost_estimate=pl.CostEstimate(flops=flops, transcendentals=0, bytes_accessed=moved),
        compiler_params=pltpu.CompilerParams(vmem_limit_bytes=VMEM_BYTES),
        **kwargs,
    )


def causal(tok):
    rows = lax.broadcasted_iota(jnp.int32, (tok, tok), 0)
    cols = lax.broadcasted_iota(jnp.int32, (tok, tok), 1)
    return rows >= cols


def exchange(x, axis):
    return lax.all_to_all(x, axis, 0, 0, tiled=True)


def first_kernel(k_ref, v_ref, w_ref, out_ref):
    peers, rows, width = out_ref.shape
    own = w_ref.shape[0]
    share = (rows - own) // 2
    for h in range(width // DH):
        kv = mm(k_ref[:, head(h)], v_ref[:, head(h)], 0, 0)
        high = kv.astype(BF16)
        low = (kv - high.astype(F32)).astype(BF16)
        for p in range(peers):
            out_ref[p, own : own + share, head(h)] = high[p * share : (p + 1) * share]
            out_ref[p, own + share :, head(h)] = low[p * share : (p + 1) * share]
    for p in range(peers):
        out_ref[p, :own, :] = w_ref[...]


def split_kernel(got_ref, weight_ref, part_ref, total_ref):
    peers, rows, width = got_ref.shape
    own = weight_ref.shape[0] // peers
    share = (rows - own) // 2
    running = jnp.zeros((share, width), F32)
    for p in range(peers):
        weight_ref[p * own : (p + 1) * own, :] = got_ref[p, :own, :]
        part_ref[p] = running
        high = got_ref[p, own : own + share, :].astype(F32)
        running = running + (high + got_ref[p, own + share :, :].astype(F32))
    for p in range(total_ref.shape[0]):
        total_ref[p] = running


def later_kernel(got_ref, sums_ref):
    running = jnp.zeros(sums_ref.shape[1:], F32)
    for s in reversed(range(sums_ref.shape[0])):
        sums_ref[s] = running.astype(BF16)
        running = running + got_ref[s].astype(F32)


def join_kernel(place_ref, totals_ref, part_ref, out_ref):
    place = place_ref[0]
    base = jnp.zeros(totals_ref.shape[1:], F32)
    for other in range(totals_ref.shape[0]):
        counts = place > other
        base = base + jnp.where(counts, totals_ref[other], 0.0)
    for p in range(part_ref.shape[0]):
        out_ref[p] = (base + part_ref[p]).astype(out_ref.dtype)


def attn_kernel(q_ref, k_ref, v_ref, attn_ref, inner_ref):
    mask = causal(q_ref.shape[0])
    for h in range(q_ref.shape[1] // DH):
        scores = mm(q_ref[:, head(h)], k_ref[:, head(h)], 1, 1)
        attn = jnp.where(mask, scores, 0.0).astype(BF16)
        attn_ref[h] = attn
        inner_ref[:, head(h)] = mm(attn, v_ref[:, head(h)], 1, 0)


def proj_kernel(scale, q_ref, prior_ref, inner_ref, top_ref, low_ref, out_ref, attn_out_ref):
    @pl.when((pl.program_id(0) == 0) & (pl.program_id(1) == 0))
    def _():
        for h in range(q_ref.shape[1] // DH):
            far = mm(q_ref[:, head(h)], prior_ref[:, head(h)], 1, 0)
            attn_out_ref[:, head(h)] = (scale * (inner_ref[:, head(h)] + far)).astype(BF16)

    for x in range(out_ref.shape[1]):
        cot = jnp.concatenate([top_ref[0, x], low_ref[0, x]], axis=0)
        term = mm(cot, attn_out_ref[...], 0, 0).astype(BF16)
        out_ref[:, x, 0] = term.reshape(out_ref.shape[0], out_ref.shape[3], out_ref.shape[4])


def grad_out_kernel(top_ref, low_ref, w_ref, q_ref, g_ref, qg_ref, acc_ref):
    step = pl.program_id(0)
    term = None
    for x in range(w_ref.shape[0]):
        cot = jnp.concatenate([top_ref[0, x], low_ref[0, x]], axis=0)
        one = mm(cot, w_ref[x, 0], 1, 0)
        term = one if term is None else term + one

    @pl.when(step == 0)
    def _():
        acc_ref[...] = term

    @pl.when(step > 0)
    def _():
        acc_ref[...] += term

    @pl.when(step == pl.num_programs(0) - 1)
    def _():
        g = acc_ref[...].astype(BF16)
        g_ref[...] = g
        for h in range(g.shape[1] // DH):
            qg_ref[head(h), :] = mm(q_ref[:, head(h)], g[:, head(h)], 0, 0).astype(BF16)


def inner_grads_kernel(scale, q_ref, k_ref, v_ref, g_ref, attn_ref, prior_ref, dq_ref, dk_ref, dv_ref):
    mask = causal(q_ref.shape[0])
    for h in range(q_ref.shape[1] // DH):
        g = g_ref[:, head(h)]
        back = jnp.where(mask, mm(g, v_ref[:, head(h)], 1, 1), 0.0).astype(BF16)
        near = mm(back, k_ref[:, head(h)], 1, 0)
        far = mm(g, prior_ref[:, head(h)], 1, 1)
        dq_ref[:, head(h)] = (scale * (near + far)).astype(BF16)
        dk_ref[:, head(h)] = mm(back, q_ref[:, head(h)], 0, 0)
        dv_ref[:, head(h)] = mm(attn_ref[h], g, 0, 0)


def outer_grads_kernel(scale, k_ref, v_ref, later_ref, near_k_ref, near_v_ref, dk_ref, dv_ref):
    for h in range(k_ref.shape[1] // DH):
        later = later_ref[head(h), :]
        far_k = mm(v_ref[:, head(h)], later, 1, 1)
        dk_ref[:, head(h)] = (scale * (near_k_ref[:, head(h)] + far_k)).astype(BF16)
        far_v = mm(k_ref[:, head(h)], later, 1, 0)
        dv_ref[:, head(h)] = (scale * (near_v_ref[:, head(h)] + far_v)).astype(BF16)


def shape(dims, dtype):
    return jax.ShapeDtypeStruct(dims, dtype)


def in_hbm(x):
    return pltpu.with_memory_space_constraint(x, pltpu.HBM)


def join(place, totals, part):
    return local_call(
        join_kernel,
        shape(part.shape, BF16),
        0,
        3 * part.size * 4,
        in_specs=[
            pl.BlockSpec(memory_space=pltpu.SMEM),
            pl.BlockSpec(memory_space=pltpu.VMEM),
            pl.BlockSpec(memory_space=pltpu.VMEM),
        ],
    )(place, totals, part)


def per_device(queries, keys, values, out_cotangent, proj_weight):
    tok, width = queries.shape
    heads = width // DH
    ny, nz = lax.axis_size("y"), lax.axis_size("z")
    nx, nc = lax.axis_size("x"), lax.axis_size("c")
    cols = out_cotangent.shape[1]
    scale = (DH * tok * ny * nz) ** -0.5
    place = lax.axis_index("y").reshape(1)
    weight_t = proj_weight.T
    own = weight_t.shape[0]
    share = DH // nz
    square = 2 * tok * DH * DH * heads
    wide = 2 * tok * tok * DH * heads
    big = tok * width

    sent = local_call(
        first_kernel, shape((nz, own + 2 * share, width), BF16), square, 3 * big
    )(in_hbm(keys), in_hbm(values), in_hbm(weight_t))
    got = exchange(sent, "z")
    weight_z, kv_part, kv_total = local_call(
        split_kernel,
        (
            shape((nz * own, width), BF16),
            shape((nz, share, width), F32),
            shape((ny, share, width), F32),
        ),
        0,
        2 * big,
    )(got)
    weight_full = lax.all_gather(weight_z, "y", axis=0, tiled=True)
    cot_own, kv_total = lax.optimization_barrier((out_cotangent, kv_total))
    cot_x = lax.all_gather(cot_own, "x")
    half = tok // 2
    cot_top = lax.all_gather(cot_x[:, :half], "c")
    cot_low = lax.all_gather(cot_x[:, half:], "c")
    attn, attn_inner = local_call(
        attn_kernel,
        (shape((heads, tok, tok), BF16), shape((tok, width), F32)),
        2 * wide,
        10 * big,
    )(queries, keys, values)
    prior = exchange(join(place, exchange(kv_total, "y"), kv_part), "z")
    prior = prior.reshape(DH, width)

    n_blocks = nx * nc

    whole = pl.BlockSpec((tok, width), lambda i: (0, 0))
    state = pl.BlockSpec((DH, width), lambda i: (0, 0))
    cot_spec = pl.BlockSpec((1, nx, half, cols), lambda i: (i, 0, 0, 0))
    by_core = pl.BlockSpec((nx, 1, cols, width), lambda i: (0, i, 0, 0))
    few = nx // 2
    cot_few = pl.BlockSpec((1, few, half, cols), lambda i, j: (i, j, 0, 0))
    same = pl.BlockSpec((tok, width), lambda i, j: (0, 0))
    proj_term = local_call(
        functools.partial(proj_kernel, scale),
        pltpu.HBM((nz, nx, nc, own, width), BF16),
        square + 2 * tok * cols * width * n_blocks,
        2 * n_blocks * cols * width,
        grid=(nc, nx // few),
        in_specs=[
            same,
            pl.BlockSpec((DH, width), lambda i, j: (0, 0)),
            same,
            cot_few,
            cot_few,
        ],
        out_specs=pl.BlockSpec((nz, few, 1, own, width), lambda i, j: (0, j, i, 0, 0)),
        scratch_shapes=[pltpu.VMEM((tok, width), BF16)],
    )(queries, prior, attn_inner, cot_top, cot_low)
    proj_term = proj_term.reshape(n_blocks * cols, width)
    proj_z = lax.psum_scatter(proj_term, "z", scatter_dimension=0, tiled=True)

    grad_out, qg = local_call(
        grad_out_kernel,
        (shape((tok, width), BF16), shape((heads * DH, DH), BF16)),
        square + 2 * tok * cols * width * n_blocks,
        2 * n_blocks * cols * width,
        grid=(nc,),
        in_specs=[cot_spec, cot_spec, by_core, whole],
        out_specs=[whole, pl.BlockSpec((heads * DH, DH), lambda i: (0, 0))],
        scratch_shapes=[pltpu.VMEM((tok, width), F32)],
    )(cot_top, cot_low, in_hbm(weight_full.reshape(nx, nc, cols, width)), queries)
    pieces = (ny * nz, heads * DH // (ny * nz), DH)
    qg_got = exchange(qg.reshape(pieces), SEQ)
    sums = local_call(later_kernel, shape(pieces, BF16), 0, 2 * big)(qg_got)
    grad_q, near_k, near_v = local_call(
        functools.partial(inner_grads_kernel, scale),
        (shape((tok, width), BF16), shape((tok, width), F32), shape((tok, width), F32)),
        4 * wide + square,
        16 * big,
    )(queries, keys, values, grad_out, attn, prior)
    later = exchange(sums, SEQ).reshape(heads * DH, DH)
    grad_k, grad_v = local_call(
        functools.partial(outer_grads_kernel, scale),
        (shape((tok, width), BF16), shape((tok, width), BF16)),
        2 * square,
        12 * big,
    )(keys, values, later, near_k, near_v)

    proj_parts = exchange(proj_z.reshape(ny, own, width), "y")
    proj_sum = jnp.sum(proj_parts.astype(F32), axis=0)
    grad_proj = (proj_sum / jnp.sqrt(F32(tok * ny * nz))).T
    return grad_q, grad_k, grad_v, grad_proj


def solution(mesh):
    seq, tp = mesh.devices.shape
    inner, cores = 8, 2
    grid = Mesh(
        mesh.devices.reshape(seq // inner, inner, tp // cores, cores), ("y", "z", "x", "c")
    )
    tokens, weight = P(SEQ, ("x", "c")), P(("x", "c"), SEQ)
    return jax.shard_map(
        per_device,
        mesh=grid,
        in_specs=(tokens, tokens, tokens, tokens, weight),
        out_specs=(tokens, tokens, tokens, weight),
        check_vma=False,
    )
```

```python
import functools

import jax
import jax.numpy as jnp
from jax import lax
from jax.experimental import pallas as pl
from jax.experimental.pallas import tpu as pltpu
from jax.sharding import Mesh, PartitionSpec as P

DH = 128
SEQ = ("y", "z")
BF16 = jnp.bfloat16
F32 = jnp.float32
VMEM_BYTES = 24 * 1024 * 1024


def mm(a, b, ca, cb):
    return lax.dot_general(a, b, (((ca,), (cb,)), ((), ())), preferred_element_type=F32)


def head(h):
    return slice(h * DH, (h + 1) * DH)


def local_call(kernel, out_shape, flops, moved, **kwargs):
    return pl.pallas_call(
        kernel,
        out_shape=out_shape,
        cost_estimate=pl.CostEstimate(flops=flops, transcendentals=0, bytes_accessed=moved),
        compiler_params=pltpu.CompilerParams(vmem_limit_bytes=VMEM_BYTES),
        **kwargs,
    )


def causal(tok):
    rows = lax.broadcasted_iota(jnp.int32, (tok, tok), 0)
    cols = lax.broadcasted_iota(jnp.int32, (tok, tok), 1)
    return rows >= cols


def exchange(x, axis):
    return lax.all_to_all(x, axis, 0, 0, tiled=True)


def first_kernel(k_ref, v_ref, w_ref, out_ref):
    peers, rows, width = out_ref.shape
    own = w_ref.shape[0]
    share = (rows - own) // 2
    for h in range(width // DH):
        kv = mm(k_ref[:, head(h)], v_ref[:, head(h)], 0, 0)
        high = kv.astype(BF16)
        low = (kv - high.astype(F32)).astype(BF16)
        for p in range(peers):
            out_ref[p, own : own + share, head(h)] = high[p * share : (p + 1) * share]
            out_ref[p, own + share :, head(h)] = low[p * share : (p + 1) * share]
    for p in range(peers):
        out_ref[p, :own, :] = w_ref[...]


def weight_kernel(got_ref, weight_ref):
    peers = got_ref.shape[0]
    own = weight_ref.shape[0] // peers
    for p in range(peers):
        weight_ref[p * own : (p + 1) * own, :] = got_ref[p, :own, :]


def part_kernel(own, got_ref, part_ref, total_ref):
    share = part_ref.shape[1]
    running = jnp.zeros(part_ref.shape[1:], F32)
    for p in range(got_ref.shape[0]):
        part_ref[p] = running
        high = got_ref[p, own : own + share, :].astype(F32)
        running = running + (high + got_ref[p, own + share :, :].astype(F32))
    for p in range(total_ref.shape[0]):
        total_ref[p] = running


def later_kernel(got_ref, sums_ref):
    running = jnp.zeros(sums_ref.shape[1:], F32)
    for s in reversed(range(sums_ref.shape[0])):
        sums_ref[s] = running.astype(BF16)
        running = running + got_ref[s].astype(F32)


def join_kernel(place_ref, totals_ref, part_ref, out_ref):
    place = place_ref[0]
    base = jnp.zeros(totals_ref.shape[1:], F32)
    for other in range(totals_ref.shape[0]):
        counts = place > other
        base = base + jnp.where(counts, totals_ref[other], 0.0)
    for p in range(part_ref.shape[0]):
        out_ref[p] = (base + part_ref[p]).astype(out_ref.dtype)


def attn_kernel(q_ref, k_ref, v_ref, attn_ref, inner_ref):
    mask = causal(q_ref.shape[0])
    for h in range(q_ref.shape[1] // DH):
        scores = mm(q_ref[:, head(h)], k_ref[:, head(h)], 1, 1)
        attn = jnp.where(mask, scores, 0.0).astype(BF16)
        attn_ref[h] = attn
        inner_ref[:, head(h)] = mm(attn, v_ref[:, head(h)], 1, 0)


def proj_kernel(scale, q_ref, prior_ref, inner_ref, top_ref, low_ref, out_ref, attn_out_ref):
    @pl.when((pl.program_id(0) == 0) & (pl.program_id(1) == 0))
    def _():
        for h in range(q_ref.shape[1] // DH):
            far = mm(q_ref[:, head(h)], prior_ref[:, head(h)], 1, 0)
            attn_out_ref[:, head(h)] = (scale * (inner_ref[:, head(h)] + far)).astype(BF16)

    for x in range(out_ref.shape[1]):
        cot = jnp.concatenate([top_ref[0, x], low_ref[0, x]], axis=0)
        term = mm(cot, attn_out_ref[...], 0, 0).astype(BF16)
        out_ref[:, x, 0] = term.reshape(out_ref.shape[0], out_ref.shape[3], out_ref.shape[4])


def grad_out_kernel(top_ref, low_ref, w_ref, q_ref, g_ref, qg_ref, acc_ref):
    step = pl.program_id(0)
    term = None
    for x in range(w_ref.shape[0]):
        cot = jnp.concatenate([top_ref[0, x], low_ref[0, x]], axis=0)
        one = mm(cot, w_ref[x, 0], 1, 0)
        term = one if term is None else term + one

    @pl.when(step == 0)
    def _():
        acc_ref[...] = term

    @pl.when(step > 0)
    def _():
        acc_ref[...] += term

    @pl.when(step == pl.num_programs(0) - 1)
    def _():
        g = acc_ref[...].astype(BF16)
        g_ref[...] = g
        for h in range(g.shape[1] // DH):
            qg_ref[head(h), :] = mm(q_ref[:, head(h)], g[:, head(h)], 0, 0).astype(BF16)


def inner_grads_kernel(scale, q_ref, k_ref, v_ref, g_ref, attn_ref, prior_ref, dq_ref, dk_ref, dv_ref):
    mask = causal(q_ref.shape[0])
    for h in range(q_ref.shape[1] // DH):
        g = g_ref[:, head(h)]
        back = jnp.where(mask, mm(g, v_ref[:, head(h)], 1, 1), 0.0).astype(BF16)
        near = mm(back, k_ref[:, head(h)], 1, 0)
        far = mm(g, prior_ref[:, head(h)], 1, 1)
        dq_ref[:, head(h)] = (scale * (near + far)).astype(BF16)
        dk_ref[:, head(h)] = mm(back, q_ref[:, head(h)], 0, 0)
        dv_ref[:, head(h)] = mm(attn_ref[h], g, 0, 0)


def outer_grads_kernel(scale, k_ref, v_ref, later_ref, near_k_ref, near_v_ref, dk_ref, dv_ref):
    for h in range(k_ref.shape[1] // DH):
        later = later_ref[head(h), :]
        far_k = mm(v_ref[:, head(h)], later, 1, 1)
        dk_ref[:, head(h)] = (scale * (near_k_ref[:, head(h)] + far_k)).astype(BF16)
        far_v = mm(k_ref[:, head(h)], later, 1, 0)
        dv_ref[:, head(h)] = (scale * (near_v_ref[:, head(h)] + far_v)).astype(BF16)


def shape(dims, dtype):
    return jax.ShapeDtypeStruct(dims, dtype)


def in_hbm(x):
    return pltpu.with_memory_space_constraint(x, pltpu.HBM)


def join(place, totals, part):
    return local_call(
        join_kernel,
        shape(part.shape, BF16),
        0,
        3 * part.size * 4,
        in_specs=[
            pl.BlockSpec(memory_space=pltpu.SMEM),
            pl.BlockSpec(memory_space=pltpu.VMEM),
            pl.BlockSpec(memory_space=pltpu.VMEM),
        ],
    )(place, totals, part)


def per_device(queries, keys, values, out_cotangent, proj_weight):
    tok, width = queries.shape
    heads = width // DH
    ny, nz = lax.axis_size("y"), lax.axis_size("z")
    nx, nc = lax.axis_size("x"), lax.axis_size("c")
    cols = out_cotangent.shape[1]
    scale = (DH * tok * ny * nz) ** -0.5
    place = lax.axis_index("y").reshape(1)
    weight_t = proj_weight.T
    own = weight_t.shape[0]
    share = DH // nz
    square = 2 * tok * DH * DH * heads
    wide = 2 * tok * tok * DH * heads
    big = tok * width

    sent = local_call(
        first_kernel, shape((nz, own + 2 * share, width), BF16), square, 3 * big
    )(in_hbm(keys), in_hbm(values), in_hbm(weight_t))
    got = exchange(sent, "z")
    weight_z = local_call(weight_kernel, shape((nz * own, width), BF16), 0, big)(got)
    got, weight_z = lax.optimization_barrier((got, weight_z))
    kv_part, kv_total = local_call(
        functools.partial(part_kernel, own),
        (shape((nz, share, width), F32), shape((ny, share, width), F32)),
        0,
        2 * big,
    )(got)
    weight_full = lax.all_gather(weight_z, "y", axis=0, tiled=True)
    cot_own, kv_total = lax.optimization_barrier((out_cotangent, kv_total))
    cot_x = lax.all_gather(cot_own, "x")
    half = tok // 2
    cot_top = lax.all_gather(cot_x[:, :half], "c")
    cot_low = lax.all_gather(cot_x[:, half:], "c")
    attn, attn_inner = local_call(
        attn_kernel,
        (shape((heads, tok, tok), BF16), shape((tok, width), F32)),
        2 * wide,
        10 * big,
    )(queries, keys, values)
    prior = exchange(join(place, exchange(kv_total, "y"), kv_part), "z")
    prior = prior.reshape(DH, width)

    n_blocks = nx * nc

    whole = pl.BlockSpec((tok, width), lambda i: (0, 0))
    state = pl.BlockSpec((DH, width), lambda i: (0, 0))
    cot_spec = pl.BlockSpec((1, nx, half, cols), lambda i: (i, 0, 0, 0))
    by_core = pl.BlockSpec((nx, 1, cols, width), lambda i: (0, i, 0, 0))
    few = nx // 2
    cot_few = pl.BlockSpec((1, few, half, cols), lambda i, j: (i, j, 0, 0))
    same = pl.BlockSpec((tok, width), lambda i, j: (0, 0))
    proj_term = local_call(
        functools.partial(proj_kernel, scale),
        pltpu.HBM((nz, nx, nc, own, width), BF16),
        square + 2 * tok * cols * width * n_blocks,
        2 * n_blocks * cols * width,
        grid=(nc, nx // few),
        in_specs=[
            same,
            pl.BlockSpec((DH, width), lambda i, j: (0, 0)),
            same,
            cot_few,
            cot_few,
        ],
        out_specs=pl.BlockSpec((nz, few, 1, own, width), lambda i, j: (0, j, i, 0, 0)),
        scratch_shapes=[pltpu.VMEM((tok, width), BF16)],
    )(queries, prior, attn_inner, cot_top, cot_low)
    proj_term = proj_term.reshape(n_blocks * cols, width)
    proj_z = lax.psum_scatter(proj_term, "z", scatter_dimension=0, tiled=True)

    turns = nx // few
    cot_step = pl.BlockSpec((1, few, half, cols), lambda i: (i // turns, i % turns, 0, 0))
    weight_step = pl.BlockSpec((few, 1, cols, width), lambda i: (i % turns, i // turns, 0, 0))
    grad_out, qg = local_call(
        grad_out_kernel,
        (shape((tok, width), BF16), shape((heads * DH, DH), BF16)),
        square + 2 * tok * cols * width * n_blocks,
        2 * n_blocks * cols * width,
        grid=(nc * (nx // few),),
        in_specs=[cot_step, cot_step, weight_step, whole],
        out_specs=[whole, pl.BlockSpec((heads * DH, DH), lambda i: (0, 0))],
        scratch_shapes=[pltpu.VMEM((tok, width), F32)],
    )(cot_top, cot_low, in_hbm(weight_full.reshape(nx, nc, cols, width)), queries)
    pieces = (ny * nz, heads * DH // (ny * nz), DH)
    qg_got = exchange(qg.reshape(pieces), SEQ)
    sums = local_call(later_kernel, shape(pieces, BF16), 0, 2 * big)(qg_got)
    grad_q, near_k, near_v = local_call(
        functools.partial(inner_grads_kernel, scale),
        (shape((tok, width), BF16), shape((tok, width), F32), shape((tok, width), F32)),
        4 * wide + square,
        16 * big,
    )(queries, keys, values, grad_out, attn, prior)
    later = exchange(sums, SEQ).reshape(heads * DH, DH)
    grad_k, grad_v = local_call(
        functools.partial(outer_grads_kernel, scale),
        (shape((tok, width), BF16), shape((tok, width), BF16)),
        2 * square,
        12 * big,
    )(keys, values, later, near_k, near_v)

    proj_parts = exchange(proj_z.reshape(ny, own, width), "y")
    proj_sum = jnp.sum(proj_parts.astype(F32), axis=0)
    grad_proj = (proj_sum / jnp.sqrt(F32(tok * ny * nz))).T
    return grad_q, grad_k, grad_v, grad_proj


def solution(mesh):
    seq, tp = mesh.devices.shape
    inner, cores = 8, 2
    grid = Mesh(
        mesh.devices.reshape(seq // inner, inner, tp // cores, cores), ("y", "z", "x", "c")
    )
    tokens, weight = P(SEQ, ("x", "c")), P(("x", "c"), SEQ)
    return jax.shard_map(
        per_device,
        mesh=grid,
        in_specs=(tokens, tokens, tokens, tokens, weight),
        out_specs=(tokens, tokens, tokens, weight),
        check_vma=False,
    )
```

```python
import functools

import jax
import jax.numpy as jnp
from jax import lax
from jax.experimental import pallas as pl
from jax.experimental.pallas import tpu as pltpu
from jax.sharding import Mesh, PartitionSpec as P

DH = 128
SEQ = ("y", "z")
BF16 = jnp.bfloat16
F32 = jnp.float32
VMEM_BYTES = 24 * 1024 * 1024


def mm(a, b, ca, cb):
    return lax.dot_general(a, b, (((ca,), (cb,)), ((), ())), preferred_element_type=F32)


def head(h):
    return slice(h * DH, (h + 1) * DH)


def local_call(kernel, out_shape, flops, moved, **kwargs):
    return pl.pallas_call(
        kernel,
        out_shape=out_shape,
        cost_estimate=pl.CostEstimate(flops=flops, transcendentals=0, bytes_accessed=moved),
        compiler_params=pltpu.CompilerParams(vmem_limit_bytes=VMEM_BYTES),
        **kwargs,
    )


def causal(tok):
    rows = lax.broadcasted_iota(jnp.int32, (tok, tok), 0)
    cols = lax.broadcasted_iota(jnp.int32, (tok, tok), 1)
    return rows >= cols


def exchange(x, axis):
    return lax.all_to_all(x, axis, 0, 0, tiled=True)


def first_kernel(k_ref, v_ref, w_ref, out_ref):
    peers, rows, width = out_ref.shape
    own = w_ref.shape[0]
    share = (rows - own) // 2
    for h in range(width // DH):
        kv = mm(k_ref[:, head(h)], v_ref[:, head(h)], 0, 0)
        high = kv.astype(BF16)
        low = (kv - high.astype(F32)).astype(BF16)
        for p in range(peers):
            out_ref[p, own : own + share, head(h)] = high[p * share : (p + 1) * share]
            out_ref[p, own + share :, head(h)] = low[p * share : (p + 1) * share]
    for p in range(peers):
        out_ref[p, :own, :] = w_ref[...]


def split_kernel(got_ref, weight_ref, part_ref, total_ref):
    peers, rows, width = got_ref.shape
    own = weight_ref.shape[0] // peers
    share = (rows - own) // 2
    running = jnp.zeros((share, width), F32)
    for p in range(peers):
        weight_ref[p * own : (p + 1) * own, :] = got_ref[p, :own, :]
        part_ref[p] = running
        high = got_ref[p, own : own + share, :].astype(F32)
        running = running + (high + got_ref[p, own + share :, :].astype(F32))
    for p in range(total_ref.shape[0]):
        total_ref[p] = running


def later_kernel(got_ref, sums_ref):
    running = jnp.zeros(sums_ref.shape[1:], F32)
    for s in reversed(range(sums_ref.shape[0])):
        sums_ref[s] = running.astype(BF16)
        running = running + got_ref[s].astype(F32)


def join_kernel(place_ref, totals_ref, part_ref, out_ref):
    place = place_ref[0]
    base = jnp.zeros(totals_ref.shape[1:], F32)
    for other in range(totals_ref.shape[0]):
        counts = place > other
        base = base + jnp.where(counts, totals_ref[other], 0.0)
    for p in range(part_ref.shape[0]):
        out_ref[p] = (base + part_ref[p]).astype(out_ref.dtype)


def attn_kernel(q_ref, k_ref, v_ref, attn_ref, inner_ref):
    mask = causal(q_ref.shape[0])
    for h in range(q_ref.shape[1] // DH):
        scores = mm(q_ref[:, head(h)], k_ref[:, head(h)], 1, 1)
        attn = jnp.where(mask, scores, 0.0).astype(BF16)
        attn_ref[h] = attn
        inner_ref[:, head(h)] = mm(attn, v_ref[:, head(h)], 1, 0)


def proj_kernel(scale, q_ref, prior_ref, inner_ref, top_ref, low_ref, out_ref, attn_out_ref):
    @pl.when((pl.program_id(0) == 0) & (pl.program_id(1) == 0))
    def _():
        for h in range(q_ref.shape[1] // DH):
            far = mm(q_ref[:, head(h)], prior_ref[:, head(h)], 1, 0)
            attn_out_ref[:, head(h)] = (scale * (inner_ref[:, head(h)] + far)).astype(BF16)

    for x in range(out_ref.shape[1]):
        cot = jnp.concatenate([top_ref[0, x], low_ref[0, x]], axis=0)
        term = mm(cot, attn_out_ref[...], 0, 0).astype(BF16)
        out_ref[:, x, 0] = term.reshape(out_ref.shape[0], out_ref.shape[3], out_ref.shape[4])


def grad_out_kernel(top_ref, low_ref, w_ref, q_ref, g_ref, qg_ref):
    total = None
    for x in range(w_ref.shape[0]):
        for c in range(w_ref.shape[1]):
            cot = jnp.concatenate([top_ref[c, x], low_ref[c, x]], axis=0)
            term = mm(cot, w_ref[x, c], 1, 0)
            total = term if total is None else total + term
    g = total.astype(BF16)
    g_ref[...] = g
    for h in range(g.shape[1] // DH):
        qg_ref[head(h), :] = mm(q_ref[:, head(h)], g[:, head(h)], 0, 0).astype(BF16)


def inner_grads_kernel(scale, q_ref, k_ref, v_ref, g_ref, attn_ref, prior_ref, dq_ref, dk_ref, dv_ref):
    mask = causal(q_ref.shape[0])
    for h in range(q_ref.shape[1] // DH):
        g = g_ref[:, head(h)]
        back = jnp.where(mask, mm(g, v_ref[:, head(h)], 1, 1), 0.0).astype(BF16)
        near = mm(back, k_ref[:, head(h)], 1, 0)
        far = mm(g, prior_ref[:, head(h)], 1, 1)
        dq_ref[:, head(h)] = (scale * (near + far)).astype(BF16)
        dk_ref[:, head(h)] = mm(back, q_ref[:, head(h)], 0, 0)
        dv_ref[:, head(h)] = mm(attn_ref[h], g, 0, 0)


def outer_grads_kernel(scale, k_ref, v_ref, later_ref, near_k_ref, near_v_ref, dk_ref, dv_ref):
    for h in range(k_ref.shape[1] // DH):
        later = later_ref[head(h), :]
        far_k = mm(v_ref[:, head(h)], later, 1, 1)
        dk_ref[:, head(h)] = (scale * (near_k_ref[:, head(h)] + far_k)).astype(BF16)
        far_v = mm(k_ref[:, head(h)], later, 1, 0)
        dv_ref[:, head(h)] = (scale * (near_v_ref[:, head(h)] + far_v)).astype(BF16)


def shape(dims, dtype):
    return jax.ShapeDtypeStruct(dims, dtype)


def in_hbm(x):
    return pltpu.with_memory_space_constraint(x, pltpu.HBM)


def join(place, totals, part):
    return local_call(
        join_kernel,
        shape(part.shape, BF16),
        0,
        3 * part.size * 4,
        in_specs=[
            pl.BlockSpec(memory_space=pltpu.SMEM),
            pl.BlockSpec(memory_space=pltpu.VMEM),
            pl.BlockSpec(memory_space=pltpu.VMEM),
        ],
    )(place, totals, part)


def per_device(queries, keys, values, out_cotangent, proj_weight):
    tok, width = queries.shape
    heads = width // DH
    ny, nz = lax.axis_size("y"), lax.axis_size("z")
    nx, nc = lax.axis_size("x"), lax.axis_size("c")
    cols = out_cotangent.shape[1]
    scale = (DH * tok * ny * nz) ** -0.5
    place = lax.axis_index("y").reshape(1)
    weight_t = proj_weight.T
    own = weight_t.shape[0]
    share = DH // nz
    square = 2 * tok * DH * DH * heads
    wide = 2 * tok * tok * DH * heads
    big = tok * width

    sent = local_call(
        first_kernel, shape((nz, own + 2 * share, width), BF16), square, 3 * big
    )(in_hbm(keys), in_hbm(values), in_hbm(weight_t))
    got = exchange(sent, "z")
    weight_z, kv_part, kv_total = local_call(
        split_kernel,
        (
            shape((nz * own, width), BF16),
            shape((nz, share, width), F32),
            shape((ny, share, width), F32),
        ),
        0,
        2 * big,
    )(got)
    weight_full = lax.all_gather(weight_z, "y", axis=0, tiled=True)
    cot_own, kv_total = lax.optimization_barrier((out_cotangent, kv_total))
    cot_x = lax.all_gather(cot_own, "x")
    half = tok // 2
    cot_top = lax.all_gather(cot_x[:, :half], "c")
    cot_low = lax.all_gather(cot_x[:, half:], "c")
    attn, attn_inner = local_call(
        attn_kernel,
        (shape((heads, tok, tok), BF16), shape((tok, width), F32)),
        2 * wide,
        10 * big,
    )(queries, keys, values)
    prior = exchange(join(place, exchange(kv_total, "y"), kv_part), "z")
    prior = prior.reshape(DH, width)

    n_blocks = nx * nc

    whole = pl.BlockSpec((tok, width), lambda i: (0, 0))
    state = pl.BlockSpec((DH, width), lambda i: (0, 0))
    cot_spec = pl.BlockSpec((1, nx, half, cols), lambda i: (i, 0, 0, 0))
    by_core = pl.BlockSpec((nx, 1, cols, width), lambda i: (0, i, 0, 0))
    few = nx
    cot_few = pl.BlockSpec((1, few, half, cols), lambda i, j: (i, j, 0, 0))
    same = pl.BlockSpec((tok, width), lambda i, j: (0, 0))
    proj_term = local_call(
        functools.partial(proj_kernel, scale),
        pltpu.HBM((nz, nx, nc, own, width), BF16),
        square + 2 * tok * cols * width * n_blocks,
        2 * n_blocks * cols * width,
        grid=(nc, nx // few),
        in_specs=[
            same,
            pl.BlockSpec((DH, width), lambda i, j: (0, 0)),
            same,
            cot_few,
            cot_few,
        ],
        out_specs=pl.BlockSpec((nz, few, 1, own, width), lambda i, j: (0, j, i, 0, 0)),
        scratch_shapes=[pltpu.VMEM((tok, width), BF16)],
    )(queries, prior, attn_inner, cot_top, cot_low)
    proj_term = proj_term.reshape(n_blocks * cols, width)
    proj_z = lax.psum_scatter(proj_term, "z", scatter_dimension=0, tiled=True)

    grad_out, qg = local_call(
        grad_out_kernel,
        (shape((tok, width), BF16), shape((heads * DH, DH), BF16)),
        square + 2 * tok * cols * width * n_blocks,
        2 * n_blocks * cols * width,
    )(cot_top, cot_low, in_hbm(weight_full.reshape(nx, nc, cols, width)), queries)
    pieces = (ny * nz, heads * DH // (ny * nz), DH)
    qg_got = exchange(qg.reshape(pieces), SEQ)
    sums = local_call(later_kernel, shape(pieces, BF16), 0, 2 * big)(qg_got)
    grad_q, near_k, near_v = local_call(
        functools.partial(inner_grads_kernel, scale),
        (shape((tok, width), BF16), shape((tok, width), F32), shape((tok, width), F32)),
        4 * wide + square,
        16 * big,
    )(queries, keys, values, grad_out, attn, prior)
    later = exchange(sums, SEQ).reshape(heads * DH, DH)
    grad_k, grad_v = local_call(
        functools.partial(outer_grads_kernel, scale),
        (shape((tok, width), BF16), shape((tok, width), BF16)),
        2 * square,
        12 * big,
    )(keys, values, later, near_k, near_v)

    proj_parts = exchange(proj_z.reshape(ny, own, width), "y")
    proj_sum = jnp.sum(proj_parts.astype(F32), axis=0)
    grad_proj = (proj_sum / jnp.sqrt(F32(tok * ny * nz))).T
    return grad_q, grad_k, grad_v, grad_proj


def solution(mesh):
    seq, tp = mesh.devices.shape
    inner, cores = 8, 2
    grid = Mesh(
        mesh.devices.reshape(seq // inner, inner, tp // cores, cores), ("y", "z", "x", "c")
    )
    tokens, weight = P(SEQ, ("x", "c")), P(("x", "c"), SEQ)
    return jax.shard_map(
        per_device,
        mesh=grid,
        in_specs=(tokens, tokens, tokens, tokens, weight),
        out_specs=(tokens, tokens, tokens, weight),
        check_vma=False,
    )
```

```python
import functools

import jax
import jax.numpy as jnp
from jax import lax
from jax.experimental import pallas as pl
from jax.experimental.pallas import tpu as pltpu
from jax.sharding import Mesh, PartitionSpec as P

DH = 128
SEQ = ("y", "z")
BF16 = jnp.bfloat16
F32 = jnp.float32
VMEM_BYTES = 24 * 1024 * 1024


def mm(a, b, ca, cb):
    return lax.dot_general(a, b, (((ca,), (cb,)), ((), ())), preferred_element_type=F32)


def head(h):
    return slice(h * DH, (h + 1) * DH)


def local_call(kernel, out_shape, flops, moved, **kwargs):
    return pl.pallas_call(
        kernel,
        out_shape=out_shape,
        cost_estimate=pl.CostEstimate(flops=flops, transcendentals=0, bytes_accessed=moved),
        compiler_params=pltpu.CompilerParams(vmem_limit_bytes=VMEM_BYTES),
        **kwargs,
    )


def causal(tok):
    rows = lax.broadcasted_iota(jnp.int32, (tok, tok), 0)
    cols = lax.broadcasted_iota(jnp.int32, (tok, tok), 1)
    return rows >= cols


def exchange(x, axis):
    return lax.all_to_all(x, axis, 0, 0, tiled=True)


def first_kernel(k_ref, v_ref, w_ref, out_ref):
    peers, rows, width = out_ref.shape
    own = w_ref.shape[0]
    share = (rows - own) // 2
    for h in range(width // DH):
        kv = mm(k_ref[:, head(h)], v_ref[:, head(h)], 0, 0)
        high = kv.astype(BF16)
        low = (kv - high.astype(F32)).astype(BF16)
        for p in range(peers):
            out_ref[p, own : own + share, head(h)] = high[p * share : (p + 1) * share]
            out_ref[p, own + share :, head(h)] = low[p * share : (p + 1) * share]
    for p in range(peers):
        out_ref[p, :own, :] = w_ref[...]


def split_kernel(got_ref, weight_ref, part_ref, total_ref):
    peers, rows, width = got_ref.shape
    own = weight_ref.shape[0] // peers
    share = (rows - own) // 2
    running = jnp.zeros((share, width), F32)
    for p in range(peers):
        weight_ref[p * own : (p + 1) * own, :] = got_ref[p, :own, :]
        part_ref[p] = running
        high = got_ref[p, own : own + share, :].astype(F32)
        running = running + (high + got_ref[p, own + share :, :].astype(F32))
    for p in range(total_ref.shape[0]):
        total_ref[p] = running


def later_kernel(got_ref, sums_ref):
    running = jnp.zeros(sums_ref.shape[1:], F32)
    for s in reversed(range(sums_ref.shape[0])):
        sums_ref[s] = running.astype(BF16)
        running = running + got_ref[s].astype(F32)


def join_kernel(place_ref, totals_ref, part_ref, out_ref):
    place = place_ref[0]
    base = jnp.zeros(totals_ref.shape[1:], F32)
    for other in range(totals_ref.shape[0]):
        counts = place > other
        base = base + jnp.where(counts, totals_ref[other], 0.0)
    for p in range(part_ref.shape[0]):
        out_ref[p] = (base + part_ref[p]).astype(out_ref.dtype)


def attn_kernel(q_ref, k_ref, v_ref, attn_ref, inner_ref):
    mask = causal(q_ref.shape[0])
    for h in range(q_ref.shape[1] // DH):
        scores = mm(q_ref[:, head(h)], k_ref[:, head(h)], 1, 1)
        attn = jnp.where(mask, scores, 0.0).astype(BF16)
        attn_ref[h] = attn
        inner_ref[:, head(h)] = mm(attn, v_ref[:, head(h)], 1, 0)


def proj_kernel(scale, q_ref, prior_ref, inner_ref, top_ref, low_ref, out_ref, attn_out_ref):
    @pl.when((pl.program_id(0) == 0) & (pl.program_id(1) == 0))
    def _():
        for h in range(q_ref.shape[1] // DH):
            far = mm(q_ref[:, head(h)], prior_ref[:, head(h)], 1, 0)
            attn_out_ref[:, head(h)] = (scale * (inner_ref[:, head(h)] + far)).astype(BF16)

    for x in range(out_ref.shape[1]):
        cot = jnp.concatenate([top_ref[0, x], low_ref[0, x]], axis=0)
        term = mm(cot, attn_out_ref[...], 0, 0).astype(BF16)
        out_ref[:, x, 0] = term.reshape(out_ref.shape[0], out_ref.shape[3], out_ref.shape[4])


def grad_out_kernel(top_ref, low_ref, w_ref, q_ref, g_ref, qg_ref):
    total = None
    for x in range(w_ref.shape[0]):
        for c in range(w_ref.shape[1]):
            cot = jnp.concatenate([top_ref[c, x], low_ref[c, x]], axis=0)
            term = mm(cot, w_ref[x, c], 1, 0)
            total = term if total is None else total + term
    g = total.astype(BF16)
    g_ref[...] = g
    for h in range(g.shape[1] // DH):
        qg_ref[head(h), :] = mm(q_ref[:, head(h)], g[:, head(h)], 0, 0).astype(BF16)


def inner_grads_kernel(scale, q_ref, k_ref, v_ref, g_ref, attn_ref, prior_ref, dq_ref, dk_ref, dv_ref):
    mask = causal(q_ref.shape[0])
    for h in range(q_ref.shape[1] // DH):
        g = g_ref[:, head(h)]
        back = jnp.where(mask, mm(g, v_ref[:, head(h)], 1, 1), 0.0).astype(BF16)
        near = mm(back, k_ref[:, head(h)], 1, 0)
        far = mm(g, prior_ref[:, head(h)], 1, 1)
        dq_ref[:, head(h)] = (scale * (near + far)).astype(BF16)
        dk_ref[:, head(h)] = mm(back, q_ref[:, head(h)], 0, 0)
        dv_ref[:, head(h)] = mm(attn_ref[h], g, 0, 0)


def outer_grads_kernel(scale, k_ref, v_ref, later_ref, near_k_ref, near_v_ref, dk_ref, dv_ref):
    for h in range(k_ref.shape[1] // DH):
        later = later_ref[head(h), :]
        far_k = mm(v_ref[:, head(h)], later, 1, 1)
        dk_ref[:, head(h)] = (scale * (near_k_ref[:, head(h)] + far_k)).astype(BF16)
        far_v = mm(k_ref[:, head(h)], later, 1, 0)
        dv_ref[:, head(h)] = (scale * (near_v_ref[:, head(h)] + far_v)).astype(BF16)


def shape(dims, dtype):
    return jax.ShapeDtypeStruct(dims, dtype)


def in_hbm(x):
    return pltpu.with_memory_space_constraint(x, pltpu.HBM)


def join(place, totals, part):
    return local_call(
        join_kernel,
        shape(part.shape, BF16),
        0,
        3 * part.size * 4,
        in_specs=[
            pl.BlockSpec(memory_space=pltpu.SMEM),
            pl.BlockSpec(memory_space=pltpu.VMEM),
            pl.BlockSpec(memory_space=pltpu.VMEM),
        ],
    )(place, totals, part)


def per_device(queries, keys, values, out_cotangent, proj_weight):
    tok, width = queries.shape
    heads = width // DH
    ny, nz = lax.axis_size("y"), lax.axis_size("z")
    nx, nc = lax.axis_size("x"), lax.axis_size("c")
    cols = out_cotangent.shape[1]
    scale = (DH * tok * ny * nz) ** -0.5
    place = lax.axis_index("y").reshape(1)
    weight_t = proj_weight.T
    own = weight_t.shape[0]
    share = DH // nz
    square = 2 * tok * DH * DH * heads
    wide = 2 * tok * tok * DH * heads
    big = tok * width

    sent = local_call(
        first_kernel, shape((nz, own + 2 * share, width), BF16), square, 3 * big
    )(in_hbm(keys), in_hbm(values), in_hbm(weight_t))
    got = exchange(sent, "z")
    weight_z, kv_part, kv_total = local_call(
        split_kernel,
        (
            shape((nz * own, width), BF16),
            shape((nz, share, width), F32),
            shape((ny, share, width), F32),
        ),
        0,
        2 * big,
    )(got)
    weight_full = lax.all_gather(weight_z, "y", axis=0, tiled=True)
    cot_own, kv_total = lax.optimization_barrier((out_cotangent, kv_total))
    cot_x = lax.all_gather(cot_own, "x")
    half = tok // 2
    cot_top = lax.all_gather(cot_x[:, :half], "c")
    cot_low = lax.all_gather(cot_x[:, half:], "c")
    attn, attn_inner = local_call(
        attn_kernel,
        (shape((heads, tok, tok), BF16), shape((tok, width), F32)),
        2 * wide,
        10 * big,
    )(queries, keys, values)
    prior = exchange(join(place, exchange(kv_total, "y"), kv_part), "z")
    prior = prior.reshape(DH, width)

    n_blocks = nx * nc

    whole = pl.BlockSpec((tok, width), lambda i: (0, 0))
    state = pl.BlockSpec((DH, width), lambda i: (0, 0))
    cot_spec = pl.BlockSpec((1, nx, half, cols), lambda i: (i, 0, 0, 0))
    by_core = pl.BlockSpec((nx, 1, cols, width), lambda i: (0, i, 0, 0))
    few = nx
    cot_few = pl.BlockSpec((1, few, half, cols), lambda i, j: (i, j, 0, 0))
    same = pl.BlockSpec((tok, width), lambda i, j: (0, 0))
    proj_term = local_call(
        functools.partial(proj_kernel, scale),
        pltpu.HBM((nz, nx, nc, own, width), BF16),
        square + 2 * tok * cols * width * n_blocks,
        2 * n_blocks * cols * width,
        grid=(nc, nx // few),
        in_specs=[
            same,
            pl.BlockSpec((DH, width), lambda i, j: (0, 0)),
            same,
            cot_few,
            cot_few,
        ],
        out_specs=pl.BlockSpec((nz, few, 1, own, width), lambda i, j: (0, j, i, 0, 0)),
        scratch_shapes=[pltpu.VMEM((tok, width), BF16)],
    )(queries, prior, attn_inner, cot_top, cot_low)
    proj_term = proj_term.reshape(n_blocks * cols, width)
    proj_z = lax.psum_scatter(proj_term, "z", scatter_dimension=0, tiled=True)

    grad_out, qg = local_call(
        grad_out_kernel,
        (shape((tok, width), BF16), shape((heads * DH, DH), BF16)),
        square + 2 * tok * cols * width * n_blocks,
        2 * n_blocks * cols * width,
    )(cot_top, cot_low, in_hbm(weight_full.reshape(nx, nc, cols, width)), queries)
    pieces = (ny * nz, heads * DH // (ny * nz), DH)
    qg_got = exchange(qg.reshape(pieces), SEQ)
    grad_q, near_k, near_v = local_call(
        functools.partial(inner_grads_kernel, scale),
        (shape((tok, width), BF16), shape((tok, width), F32), shape((tok, width), F32)),
        4 * wide + square,
        16 * big,
    )(queries, keys, values, grad_out, attn, prior)
    qg_got, near_k, near_v = lax.optimization_barrier((qg_got, near_k, near_v))
    sums = local_call(later_kernel, shape(pieces, BF16), 0, 2 * big)(qg_got)
    later = exchange(sums, SEQ).reshape(heads * DH, DH)
    grad_k, grad_v = local_call(
        functools.partial(outer_grads_kernel, scale),
        (shape((tok, width), BF16), shape((tok, width), BF16)),
        2 * square,
        12 * big,
    )(keys, values, later, near_k, near_v)

    proj_parts = exchange(proj_z.reshape(ny, own, width), "y")
    proj_sum = jnp.sum(proj_parts.astype(F32), axis=0)
    grad_proj = (proj_sum / jnp.sqrt(F32(tok * ny * nz))).T
    return grad_q, grad_k, grad_v, grad_proj


def solution(mesh):
    seq, tp = mesh.devices.shape
    inner, cores = 8, 2
    grid = Mesh(
        mesh.devices.reshape(seq // inner, inner, tp // cores, cores), ("y", "z", "x", "c")
    )
    tokens, weight = P(SEQ, ("x", "c")), P(("x", "c"), SEQ)
    return jax.shard_map(
        per_device,
        mesh=grid,
        in_specs=(tokens, tokens, tokens, tokens, weight),
        out_specs=(tokens, tokens, tokens, weight),
        check_vma=False,
    )
```

```python
import functools

import jax
import jax.numpy as jnp
from jax import lax
from jax.experimental import pallas as pl
from jax.experimental.pallas import tpu as pltpu
from jax.sharding import Mesh, PartitionSpec as P

DH = 128
SEQ = ("y", "z")
BF16 = jnp.bfloat16
F32 = jnp.float32
VMEM_BYTES = 24 * 1024 * 1024


def mm(a, b, ca, cb):
    return lax.dot_general(a, b, (((ca,), (cb,)), ((), ())), preferred_element_type=F32)


def head(h):
    return slice(h * DH, (h + 1) * DH)


def local_call(kernel, out_shape, flops, moved, **kwargs):
    return pl.pallas_call(
        kernel,
        out_shape=out_shape,
        cost_estimate=pl.CostEstimate(flops=flops, transcendentals=0, bytes_accessed=moved),
        compiler_params=pltpu.CompilerParams(vmem_limit_bytes=VMEM_BYTES),
        **kwargs,
    )


def causal(tok):
    rows = lax.broadcasted_iota(jnp.int32, (tok, tok), 0)
    cols = lax.broadcasted_iota(jnp.int32, (tok, tok), 1)
    return rows >= cols


def exchange(x, axis):
    return lax.all_to_all(x, axis, 0, 0, tiled=True)


def first_kernel(k_ref, v_ref, w_ref, out_ref):
    peers, rows, width = out_ref.shape
    own = w_ref.shape[0]
    share = (rows - own) // 2
    for h in range(width // DH):
        kv = mm(k_ref[:, head(h)], v_ref[:, head(h)], 0, 0)
        high = kv.astype(BF16)
        low = (kv - high.astype(F32)).astype(BF16)
        for p in range(peers):
            out_ref[p, own : own + share, head(h)] = high[p * share : (p + 1) * share]
            out_ref[p, own + share :, head(h)] = low[p * share : (p + 1) * share]
    for p in range(peers):
        out_ref[p, :own, :] = w_ref[...]


def split_kernel(got_ref, weight_ref, part_ref, total_ref):
    peers, rows, width = got_ref.shape
    own = weight_ref.shape[0] // peers
    share = (rows - own) // 2
    running = jnp.zeros((share, width), F32)
    for p in range(peers):
        weight_ref[p * own : (p + 1) * own, :] = got_ref[p, :own, :]
        part_ref[p] = running
        high = got_ref[p, own : own + share, :].astype(F32)
        running = running + (high + got_ref[p, own + share :, :].astype(F32))
    for p in range(total_ref.shape[0]):
        total_ref[p] = running


def later_kernel(got_ref, sums_ref):
    running = jnp.zeros(sums_ref.shape[1:], F32)
    for s in reversed(range(sums_ref.shape[0])):
        sums_ref[s] = running.astype(BF16)
        running = running + got_ref[s].astype(F32)


def join_kernel(place_ref, totals_ref, part_ref, out_ref):
    place = place_ref[0]
    base = jnp.zeros(totals_ref.shape[1:], F32)
    for other in range(totals_ref.shape[0]):
        counts = place > other
        base = base + jnp.where(counts, totals_ref[other], 0.0)
    for p in range(part_ref.shape[0]):
        out_ref[p] = (base + part_ref[p]).astype(out_ref.dtype)


def attn_kernel(q_ref, k_ref, v_ref, attn_ref, inner_ref):
    mask = causal(q_ref.shape[0])
    for h in range(q_ref.shape[1] // DH):
        scores = mm(q_ref[:, head(h)], k_ref[:, head(h)], 1, 1)
        attn = jnp.where(mask, scores, 0.0).astype(BF16)
        attn_ref[h] = attn
        inner_ref[:, head(h)] = mm(attn, v_ref[:, head(h)], 1, 0)


def proj_kernel(scale, q_ref, prior_ref, inner_ref, top_ref, low_ref, out_ref, attn_out_ref):
    @pl.when((pl.program_id(0) == 0) & (pl.program_id(1) == 0))
    def _():
        for h in range(q_ref.shape[1] // DH):
            far = mm(q_ref[:, head(h)], prior_ref[:, head(h)], 1, 0)
            attn_out_ref[:, head(h)] = (scale * (inner_ref[:, head(h)] + far)).astype(BF16)

    for x in range(out_ref.shape[1]):
        cot = jnp.concatenate([top_ref[0, x], low_ref[0, x]], axis=0)
        term = mm(cot, attn_out_ref[...], 0, 0).astype(BF16)
        out_ref[:, x, 0] = term.reshape(out_ref.shape[0], out_ref.shape[3], out_ref.shape[4])


def grad_out_kernel(top_ref, low_ref, w_ref, q_ref, g_ref, qg_ref):
    total = None
    for x in range(w_ref.shape[0]):
        for c in range(w_ref.shape[1]):
            cot = jnp.concatenate([top_ref[c, x], low_ref[c, x]], axis=0)
            term = mm(cot, w_ref[x, c], 1, 0)
            total = term if total is None else total + term
    g = total.astype(BF16)
    g_ref[...] = g
    for h in range(g.shape[1] // DH):
        qg_ref[head(h), :] = mm(q_ref[:, head(h)], g[:, head(h)], 0, 0).astype(BF16)


def inner_grads_kernel(scale, q_ref, k_ref, v_ref, g_ref, attn_ref, prior_ref, dq_ref, dk_ref, dv_ref):
    mask = causal(q_ref.shape[0])
    for h in range(q_ref.shape[1] // DH):
        g = g_ref[:, head(h)]
        back = jnp.where(mask, mm(g, v_ref[:, head(h)], 1, 1), 0.0).astype(BF16)
        near = mm(back, k_ref[:, head(h)], 1, 0)
        far = mm(g, prior_ref[:, head(h)], 1, 1)
        dq_ref[:, head(h)] = (scale * (near + far)).astype(BF16)
        dk_ref[:, head(h)] = mm(back, q_ref[:, head(h)], 0, 0)
        dv_ref[:, head(h)] = mm(attn_ref[h], g, 0, 0)


def outer_grads_kernel(scale, k_ref, v_ref, later_ref, near_k_ref, near_v_ref, dk_ref, dv_ref):
    for h in range(k_ref.shape[1] // DH):
        later = later_ref[head(h), :]
        far_k = mm(v_ref[:, head(h)], later, 1, 1)
        dk_ref[:, head(h)] = (scale * (near_k_ref[:, head(h)] + far_k)).astype(BF16)
        far_v = mm(k_ref[:, head(h)], later, 1, 0)
        dv_ref[:, head(h)] = (scale * (near_v_ref[:, head(h)] + far_v)).astype(BF16)


def shape(dims, dtype):
    return jax.ShapeDtypeStruct(dims, dtype)


def in_hbm(x):
    return pltpu.with_memory_space_constraint(x, pltpu.HBM)


def join(place, totals, part):
    return local_call(
        join_kernel,
        shape(part.shape, BF16),
        0,
        3 * part.size * 4,
        in_specs=[
            pl.BlockSpec(memory_space=pltpu.SMEM),
            pl.BlockSpec(memory_space=pltpu.VMEM),
            pl.BlockSpec(memory_space=pltpu.VMEM),
        ],
    )(place, totals, part)


def per_device(queries, keys, values, out_cotangent, proj_weight):
    tok, width = queries.shape
    heads = width // DH
    ny, nz = lax.axis_size("y"), lax.axis_size("z")
    nx, nc = lax.axis_size("x"), lax.axis_size("c")
    cols = out_cotangent.shape[1]
    scale = (DH * tok * ny * nz) ** -0.5
    place = lax.axis_index("y").reshape(1)
    weight_t = proj_weight.T
    own = weight_t.shape[0]
    share = DH // nz
    square = 2 * tok * DH * DH * heads
    wide = 2 * tok * tok * DH * heads
    big = tok * width

    sent = local_call(
        first_kernel, shape((nz, own + 2 * share, width), BF16), square, 3 * big
    )(in_hbm(keys), in_hbm(values), in_hbm(weight_t))
    got = exchange(sent, "z")
    weight_z, kv_part, kv_total = local_call(
        split_kernel,
        (
            shape((nz * own, width), BF16),
            shape((nz, share, width), F32),
            shape((ny, share, width), F32),
        ),
        0,
        2 * big,
    )(got)
    weight_full = lax.all_gather(weight_z, "y", axis=0, tiled=True)
    cot_own, kv_total = lax.optimization_barrier((out_cotangent, kv_total))
    cot_x = lax.all_gather(cot_own, "x")
    half = tok // 2
    cot_top = lax.all_gather(cot_x[:, :half], "c")
    cot_low = lax.all_gather(cot_x[:, half:], "c")
    attn, attn_inner = local_call(
        attn_kernel,
        (shape((heads, tok, tok), BF16), shape((tok, width), F32)),
        2 * wide,
        10 * big,
    )(queries, keys, values)
    prior = exchange(join(place, exchange(kv_total, "y"), kv_part), "z")
    prior = prior.reshape(DH, width)

    n_blocks = nx * nc

    whole = pl.BlockSpec((tok, width), lambda i: (0, 0))
    state = pl.BlockSpec((DH, width), lambda i: (0, 0))
    cot_spec = pl.BlockSpec((1, nx, half, cols), lambda i: (i, 0, 0, 0))
    by_core = pl.BlockSpec((nx, 1, cols, width), lambda i: (0, i, 0, 0))
    few = nx
    cot_few = pl.BlockSpec((1, few, half, cols), lambda i, j: (i, j, 0, 0))
    same = pl.BlockSpec((tok, width), lambda i, j: (0, 0))
    proj_term = local_call(
        functools.partial(proj_kernel, scale),
        pltpu.HBM((nz, nx, nc, own, width), BF16),
        square + 2 * tok * cols * width * n_blocks,
        2 * n_blocks * cols * width,
        grid=(nc, nx // few),
        in_specs=[
            same,
            pl.BlockSpec((DH, width), lambda i, j: (0, 0)),
            same,
            cot_few,
            cot_few,
        ],
        out_specs=pl.BlockSpec((nz, few, 1, own, width), lambda i, j: (0, j, i, 0, 0)),
        scratch_shapes=[pltpu.VMEM((tok, width), BF16)],
    )(queries, prior, attn_inner, cot_top, cot_low)
    proj_term = proj_term.reshape(n_blocks * cols, width)
    proj_z = lax.psum_scatter(proj_term, "z", scatter_dimension=0, tiled=True)

    grad_out, qg = local_call(
        grad_out_kernel,
        (shape((tok, width), BF16), shape((heads * DH, DH), BF16)),
        square + 2 * tok * cols * width * n_blocks,
        2 * n_blocks * cols * width,
    )(cot_top, cot_low, in_hbm(weight_full.reshape(nx, nc, cols, width)), queries)
    pieces = (ny * nz, heads * DH // (ny * nz), DH)
    qg_got = exchange(qg.reshape(pieces), SEQ)
    grad_q, near_k, near_v = local_call(
        functools.partial(inner_grads_kernel, scale),
        (shape((tok, width), BF16), shape((tok, width), F32), shape((tok, width), F32)),
        4 * wide + square,
        16 * big,
    )(queries, keys, values, grad_out, attn, prior)
    sums = local_call(later_kernel, shape(pieces, BF16), 0, 2 * big)(qg_got)
    later = exchange(sums, SEQ).reshape(heads * DH, DH)
    later, near_k, near_v, proj_z = lax.optimization_barrier((later, near_k, near_v, proj_z))
    grad_k, grad_v = local_call(
        functools.partial(outer_grads_kernel, scale),
        (shape((tok, width), BF16), shape((tok, width), BF16)),
        2 * square,
        12 * big,
    )(keys, values, later, near_k, near_v)

    proj_parts = exchange(proj_z.reshape(ny, own, width), "y")
    proj_sum = jnp.sum(proj_parts.astype(F32), axis=0)
    grad_proj = (proj_sum / jnp.sqrt(F32(tok * ny * nz))).T
    return grad_q, grad_k, grad_v, grad_proj


def solution(mesh):
    seq, tp = mesh.devices.shape
    inner, cores = 8, 2
    grid = Mesh(
        mesh.devices.reshape(seq // inner, inner, tp // cores, cores), ("y", "z", "x", "c")
    )
    tokens, weight = P(SEQ, ("x", "c")), P(("x", "c"), SEQ)
    return jax.shard_map(
        per_device,
        mesh=grid,
        in_specs=(tokens, tokens, tokens, tokens, weight),
        out_specs=(tokens, tokens, tokens, weight),
        check_vma=False,
    )
```
